128 devices in a mesh: row: 16 (over y, x), col: 8 (over z, core).
Axes of the slice: x: 4, y: 4, z: 4, core: 2. Of those that a mesh axis runs over, the one named last changes fastest.
Arguments:
- three_centre: float32 [16, 1024, 18432], P('row', None, 'col'), may hold values from -6 to 6
- occupied: float32 [16, 1024, 128], P('row'), may hold values from -0.1875 to 0.1875
- virtual: float32 [16, 1024, 128], P('row'), may hold values from -0.00390625 to 0.00390625
- tile_map: int32 [16, 144], P('row', 'col'), may hold values from 0 to 1, as said below
Outputs:
- polarizability: float32 [18432, 18432], P('row', 'col')
The draws below stay inside these ranges and needn't reach their ends.
Inputs may be any that keep to these rules, and one draw needn't show every extreme that they name: `tile_map`: 0 or 1; the share of ones differs from orbital to orbital.
All inputs are finite; a program needn't handle non-finite values.
Results may differ from the reference program's by a relative error of at most 0.000071.
Values sent between devices are 32-bit elements; how exact they have to be, the bound alone decides.
A program may use at most 128 MiB of HBM per device.

```python
import jax
import jax.numpy as jnp
from jax import lax

AUX = 18432
AB = 128
NB = 1024
NU = 128
MU = 16
PAIRS = 2048
NAB = 144


def draw_tile_map(key, part):
    filling_key, ticket_key = jax.random.split(jax.random.fold_in(key, 7))
    filling = jax.random.randint(filling_key, (MU, 1), 1, 5)
    ticket = jax.random.randint(ticket_key, (MU, NAB), 0, 5)
    return (ticket < filling).astype(jnp.int32)


def levels(own_key, extent, cuts, low, top_value):
    gain, own = 1.0, jax.random.fold_in(own_key, 6)
    for axis_at, parts in cuts:
        draws = jnp.exp(jax.random.uniform(jax.random.fold_in(own, axis_at), (parts,), jnp.float32, low / len(cuts), top_value / len(cuts)))
        gain = gain * jnp.repeat(draws, extent[axis_at] // parts).reshape([-1 if axis == axis_at else 1 for axis in range(len(extent))])
    return gain


def bell_draw(rng, extent, deviation, most, cuts=(), held_as=jnp.bfloat16):
    array = deviation * jax.random.normal(rng, extent, jnp.float32)
    if cuts:
        array = array * levels(rng, extent, cuts, -0.22, 0.18)
    return jnp.clip(array, -most, most).astype(held_as)


def setup_inputs(seed: int = 0) -> dict:
    arg_keys = jax.random.split(jax.random.key(seed), 5)
    return {
        "three_centre": bell_draw(arg_keys[0], (MU, NB, AUX), 1.0, 6.0, ((0, 16), (2, 8)), jnp.float32),
        "occupied": bell_draw(arg_keys[1], (MU, NB, NU), NB ** -0.5, 0.1875, ((0, 16),), jnp.float32),
        "virtual": bell_draw(arg_keys[2], (MU, NB, NU), (NB * PAIRS) ** -0.5, 0.00390625, ((0, 16),), jnp.float32),
        "tile_map": draw_tile_map(jax.random.fold_in(arg_keys[4], 71), 0),
    }


def contract_pairs(density, tensor):
    product = jnp.einsum("mnl,mnp->mlp", density, tensor, precision=lax.Precision.HIGHEST)
    return product.reshape(product.shape[0] * product.shape[1], product.shape[2])


def reference(three_centre, occupied, virtual, tile_map):
    keep_factor = jnp.repeat(tile_map.astype(jnp.float32), AB, axis=1)
    masked = three_centre * keep_factor[:, None, :]
    occupied_pairs = contract_pairs(occupied.astype(jnp.float32), masked)
    virtual_pairs = contract_pairs(virtual.astype(jnp.float32), masked)
    return lax.dot_general(occupied_pairs, virtual_pairs, (((0,), (0,)), ((), ())), precision=lax.Precision.HIGHEST, preferred_element_type=jnp.float32)
```

```python
import functools

import jax
import jax.numpy as jnp
from jax import lax
from jax.experimental import pallas as pl
from jax.experimental.pallas import tpu as pltpu
from jax.sharding import PartitionSpec as P

MESH = pl.DeviceIdType.MESH
F32, BF16 = jnp.float32, jnp.bfloat16
HALF_BLOCKS = 9
TILES = 16 * HALF_BLOCKS
WIDE = 384
PAIRS = 128
CAPS = (72, 80, 88, 96, TILES)


def place():
    row, col = lax.axis_index("row"), lax.axis_index("col")
    return row // 4, lax.rem(row, 4), col // 2, lax.rem(col, 2)


def device(y, x, z, core):
    return (y * 4 + x, z * 2 + core)


def turn(i, d):
    return lax.rem(i + (d + 4), 4)


def split(x):
    high = x.astype(BF16)
    return high, (x - high.astype(F32)).astype(BF16)


def dot3(ah, al, bh, bl):
    dot = functools.partial(jnp.dot, preferred_element_type=F32)
    return dot(ah, bh) + dot(ah, bl) + dot(al, bh)


def remote(src, dst, send, recv, target):
    return pltpu.make_async_remote_copy(
        src_ref=src, dst_ref=dst, send_sem=send, recv_sem=recv, device_id=target, device_id_type=MESH
    )


def signal(target):
    pl.semaphore_signal(pltpu.get_barrier_semaphore(), inc=1, device_id=target, device_id_type=MESH)


def spread_kernel(
    map_hbm, t_ref, occ_hbm, vir_hbm, v2_ref, op_ref, maps_ref, sums_ref,
    map_ref, occ_ref, vir_ref, tbuf, dh, dl, vbuf, obuf, v1, maps, sums,
    ox, oz, isem, tsem, s1, r1, s2, r2, loc, osend, orecv, ms, mr, ss, sr,
):
    y, x, z, core = place()
    me_row, me_col = y * 4 + x, z * 2 + core
    barrier = pltpu.get_barrier_semaphore()

    loads = [
        pltpu.make_async_copy(t_ref.at[:, pl.ds(i * WIDE, WIDE)], tbuf.at[i], tsem.at[i]) for i in range(6)
    ]
    small = [
        pltpu.make_async_copy(src, dst, isem.at[i])
        for i, (src, dst) in enumerate(((occ_hbm, occ_ref), (vir_hbm, vir_ref), (map_hbm, map_ref)))
    ]
    for load in small + loads:
        load.start()

    for d in (1, 2, 3):
        signal(device(y, turn(x, d), z, core))
        signal(device(turn(y, d), x, z, core))
    for d in range(1, 8):
        signal((me_row, lax.rem(me_col + d, 8)))
    parity = (lax.rem(x, 2), lax.rem(z, 2), lax.rem(y, 2))
    slot = (x // 2, z // 2, y // 2)

    def pair(i):
        return 2 * i + core

    targets = (
        [device(y, 2 * core + i, z, parity[0]) for i in range(2)],
        [device(y, x, pair(i), parity[1]) for i in range(2)],
        [device(pair(i), x, z, parity[2]) for i in range(2)],
    )
    sources = (
        [device(y, pair(i), z, x // 2) for i in range(2)],
        [device(y, x, pair(i), parity[1]) for i in range(2)],
        [device(pair(i), x, z, parity[2]) for i in range(2)],
    )

    def is_me(target):
        return (target[0] == me_row) & (target[1] == me_col)

    for stage in range(3):
        for source in sources[stage]:

            @pl.when(jnp.logical_not(is_me(source)))
            def _():
                signal(source)

    stays = [[is_me(target) for target in line] for line in targets]
    route = (obuf, ox, oz, op_ref)

    def piece(stage, i, q):
        spot = route[stage + 1].at[slot[stage], q]
        recv = orecv.at[stage, slot[stage], q]
        return remote(route[stage].at[i, q], spot, osend.at[stage, i, q], recv, targets[stage][i])

    def piece_start(stage, i, q):
        @pl.when(stays[stage][i])
        def _():
            spot = route[stage + 1].at[slot[stage], q]
            pltpu.make_async_copy(route[stage].at[i, q], spot, orecv.at[stage, slot[stage], q]).start()

        @pl.when(jnp.logical_not(stays[stage][i]))
        def _():
            piece(stage, i, q).start()

    def piece_arrived(stage, i, q):
        spot = route[stage + 1].at[i, q]
        pltpu.make_async_copy(spot, spot, orecv.at[stage, i, q]).wait()

    for part, ref in enumerate((occ_ref, vir_ref)):
        small[part].wait()
        high, low = split(ref[...].T)
        dh[pl.ds(part * PAIRS, PAIRS), :] = high
        dl[pl.ds(part * PAIRS, PAIRS), :] = low

    small[2].wait()
    lane = lax.broadcasted_iota(jnp.int32, (8, 128), 1)
    mine = jnp.zeros((8, 128), jnp.int32)
    for b in range(2 * HALF_BLOCKS):
        mine = jnp.where(lane == b, map_ref[0, b], mine)
    maps[y, x] = mine

    pl.semaphore_wait(barrier, 13 + sum(jnp.where(stay, 0, 1) for line in stays for stay in line))

    told = []
    for d in (1, 2, 3):
        told.append(
            remote(maps.at[y, x], maps.at[y, x], ms.at[0, d - 1], mr.at[0, d - 1], device(y, turn(x, d), z, core))
        )
        told[-1].start()

    first = []
    for h in range(2):
        for q in range(3):
            loads[3 * h + q].wait()

        def chunk(q, _):
            th, tl = split(tbuf[3 * h + q])
            r = dot3(dh[...], dl[...], th, tl)
            for b in range(3):
                keep = map_ref[0, HALF_BLOCKS * h + 3 * q + b].astype(F32)
                cut = slice(b * 128, b * 128 + 128)
                obuf[h, q, :, cut] = r[:PAIRS, cut] * keep
                vbuf[h, 3 * q + b] = r[PAIRS:, cut] * keep
            return 0

        lax.fori_loop(0, 3, chunk, 0)

        if h == 0:
            for copy in told:
                copy.wait_recv()
            for d in (1, 2, 3):
                told.append(
                    remote(maps.at[y], maps.at[y], ms.at[1, d - 1], mr.at[1, d - 1], device(turn(y, d), x, z, core))
                )
                told[-1].start()

        for q in range(3):
            piece_start(0, h, q)

        here = y if h else x
        sends = []
        for d in (1, 2, 3):
            to = turn(here, d)
            copy = remote(
                vbuf.at[h, :, pl.ds(pl.multiple_of(to * 32, 32), 32), :],
                v1.at[h, here],
                s1.at[h, d - 1],
                r1.at[h, d - 1],
                device(to, x, z, core) if h else device(y, to, z, core),
            )
            copy.start()
            sends.append(copy)
        first.append(sends)
        v1[h, here] = vbuf[h, :, pl.ds(pl.multiple_of(here * 32, 32), 32), :]

    for copy in told[3:]:
        copy.wait_recv()
    sums[me_col] = jnp.sum(maps[...].reshape(16, 8, 128), axis=0)
    for d in range(1, 8):
        told.append(
            remote(
                sums.at[me_col], sums.at[me_col], ss.at[d - 1], sr.at[d - 1], (me_row, lax.rem(me_col + d, 8))
            )
        )
        told[-1].start()

    second = []
    for h in range(2):
        for copy in first[h]:
            copy.wait_recv()
        here = x if h else y
        spot = v2_ref.at[1, :, x] if h else v2_ref.at[0, y]
        for d in (1, 2, 3):
            to = turn(here, d)
            copy = remote(
                v1.at[h, :, :, pl.ds(pl.multiple_of(to * 8, 8), 8), :],
                spot,
                s2.at[h, d - 1],
                r2.at[h, d - 1],
                device(y, to, z, core) if h else device(to, x, z, core),
            )
            copy.start()
            second.append(copy)
        copy = pltpu.make_async_copy(
            v1.at[h, :, :, pl.ds(pl.multiple_of(here * 8, 8), 8), :], spot, loc.at[h]
        )
        copy.start()
        second.append(copy)

        for q in range(3):
            for i in range(2):
                piece_arrived(h, i, q)
                piece_start(h + 1, i, q)

    for copy in told[6:]:
        copy.wait_recv()
    maps_ref[...] = maps[...].reshape(16, 8, 128)
    sums_ref[...] = sums[...]
    for copy in told:
        copy.wait_send()
    for i in range(2):
        for q in range(3):
            piece_arrived(2, i, q)
    for copy in second:
        copy.wait()
    for h in range(2):
        for copy in first[h]:
            copy.wait_send()
    for stage in range(3):
        for i in range(2):

            @pl.when(jnp.logical_not(stays[stage][i]))
            def _():
                for q in range(3):
                    piece(stage, i, q).wait_send()


def join_kernel(
    cap, table_hbm, v2_hbm, op_ref, out_ref, table, v2_ref,
    g00, g01, g02, g03, g10, g11, g12, g13, oall, lh, ll, rh, rl, acc,
    p1s, p1r, p2s, p2r, zs, zr, bs, br, loc, osem, isem,
):
    y, x, z, core = place()
    small = [pltpu.make_async_copy(table_hbm, table, isem.at[0]), pltpu.make_async_copy(v2_hbm, v2_ref, isem.at[1])]
    for load in small:
        load.start()
    barrier = pltpu.get_barrier_semaphore()
    got = ((g00, g01, g02, g03), (g10, g11, g12, g13))
    near = (
        device(y, turn(x, 1), z, core), device(y, turn(x, -1), z, core),
        device(turn(y, 1), x, z, core), device(turn(y, -1), x, z, core),
        device(y, x, turn(z, 1), core), device(y, x, turn(z, -1), core),
        device(y, x, z, 1 - core),
    )
    for target in near:
        signal(target)
    pl.semaphore_wait(barrier, len(near))
    x_next, x_last, y_next, y_last, z_next, z_last, twin = near
    sent = []

    def go(make):
        make().start()
        sent.append(make)
        return make

    zslot = (z, turn(z, -1), turn(z, 1), turn(z, 2))
    zcopy, bcopy = {}, {}
    for c in range(3):

        def first(send, recv, n, target, c=c):
            return go(lambda: remote(op_ref.at[:, c], oall.at[c, core, z], send.at[c, n], recv.at[c, n], target))

        zcopy[c, 0] = first(zs, zr, 0, z_next)
        zcopy[c, 1] = first(zs, zr, 1, z_last)
        bcopy[c, 0] = first(bs, br, 0, twin)
        pltpu.make_async_copy(op_ref.at[:, c], oall.at[c, core, z], loc.at[c]).start()

    def relay(c, n, part, target):
        def make():
            spot = oall.at[c, core, zslot[n], part]
            return remote(spot, spot, zs.at[c, n + 1], zr.at[c, n + 1], target)

        zcopy[c, n + 1] = go(make)

    def share(c, n):
        def make():
            spot = oall.at[c, core, zslot[n]]
            return remote(spot, spot, bs.at[c, n], br.at[c, n], twin)

        bcopy[c, n] = go(make)

    def occupied_near(c):
        for n, target in ((1, z_next), (2, z_last)):
            zcopy[c, n - 1]().wait_recv()
            relay(c, n, n - 1, target)
            share(c, n)

    def occupied_far(c):
        zcopy[c, 2]().wait_recv()
        zcopy[c, 3]().wait_recv()
        share(c, 3)

    def left(c):
        pltpu.make_async_copy(op_ref.at[:, c], oall.at[c, core, z], loc.at[c]).wait()
        for n in range(4):
            bcopy[c, n]().wait_recv()

        def rows(g, _):
            for j in range(4):
                t = oall[c, :, :, :, pl.ds(pl.multiple_of(g * 32, 32) + j * 8, 8), :]
                high, low = split(t.reshape(128, WIDE).T)
                lh[c, g, :, j * 128 : j * 128 + 128] = high
                ll[c, g, :, j * 128 : j * 128 + 128] = low
            return 0

        lax.fori_loop(0, 4, rows, 0)

    around = ((turn(y, -1), turn(y, 1)), (turn(x, -1), turn(x, 1)))
    axes = ((x, y, x_next, x_last, y_next, y_last), (y, x, y_next, y_last, x_next, x_last))
    half_cap = cap // 2
    whole, low_part, high_part = pl.ds(0, cap), pl.ds(0, half_cap), pl.ds(half_cap, cap - half_cap)
    p1, p2 = {}, {}
    for load in small:
        load.wait()

    def line_send(h, k, n, there, part):
        b, target = axes[h][1], axes[h][2 + k % 2]

        def make():
            return remote(
                got[h][n].at[b, part], got[h][there].at[b, part], p1s.at[h, k], p1r.at[h, k], target
            )

        p1[h, k] = go(make)

    for h in range(2):
        b = axes[h][1]

        def pack(i, _):
            for u in range(8):
                got[h][0][b, i * 8 + u] = v2_ref[h, table[h, i * 8 + u]]
            return 0

        lax.fori_loop(0, cap // 8, pack, 0)
        line_send(h, 0, 0, 1, whole)
        line_send(h, 1, 0, 2, whole)

    def line_near(h):
        p1[h, 0]().wait_recv()
        line_send(h, 2, 1, 3, low_part)
        p1[h, 1]().wait_recv()
        line_send(h, 3, 2, 3, high_part)

    def plane_move(h, n, k, at, part):
        target = axes[h][4 + k % 2]

        def make():
            spot = got[h][n].at[at, part]
            return remote(spot, spot, p2s.at[h, n, k], p2r.at[h, n, k], target)

        p2[h, n, k] = go(make)

    def plane_send(h, n):
        if n == 3:
            p1[h, 2]().wait_recv()
            p1[h, 3]().wait_recv()
        plane_move(h, n, 0, axes[h][1], whole)
        plane_move(h, n, 1, axes[h][1], whole)

    def plane_near(h, n):
        p2[h, n, 0]().wait_recv()
        plane_move(h, n, 2, around[h][0], low_part)
        p2[h, n, 1]().wait_recv()
        plane_move(h, n, 3, around[h][1], high_part)

    def right(h, n):
        p2[h, n, 2]().wait_recv()
        p2[h, n, 3]().wait_recv()

        def columns(q, _):
            for j in range(4):
                tiles = []
                for kk in range(2):
                    for zz in range(4):
                        for i in range(2):
                            m = (2 * i + kk) * 4 + zz
                            t = m * HALF_BLOCKS + q
                            tiles.append(got[h][n][j, table[2 + h, t]] * table[4 + h, t].astype(F32))
                high, low = split(jnp.concatenate(tiles, axis=0))
                cut = pl.ds(pl.multiple_of(q * 128, 128), 128)
                rh[n % 2, h, j * 128 : j * 128 + 128, cut] = high
                rl[n % 2, h, j * 128 : j * 128 + 128, cut] = low
            return 0

        lax.fori_loop(0, HALF_BLOCKS, columns, 0)

    def stage0():
        for h in both:
            line_near(h)
            plane_send(h, 0)
        occupied_near(0)
        for h in both:
            plane_near(h, 0)
            plane_send(h, 1)
        occupied_far(0)
        occupied_near(1)
        left(0)
        for h in both:
            plane_near(h, 1)
            plane_send(h, 2)
        for h in both:
            right(h, 0)

    def stage1():
        occupied_far(1)
        occupied_near(2)
        left(1)

    def stage2():
        for h in both:
            plane_near(h, 2)
            plane_send(h, 3)
        for h in both:
            right(h, 1)

    def stage3():
        occupied_far(2)
        left(2)

    def stage4():
        for h in both:
            plane_near(h, 3)
        for h in both:
            right(h, 2)

    def stage5():
        for h in both:
            right(h, 3)

    both = range(2)

    def clear(i, _):
        acc[pl.ds(pl.multiple_of(i * 64, 64), 64), :] = jnp.zeros((64, 6 * WIDE), F32)
        return 0

    lax.fori_loop(0, 18, clear, 0)

    def run(s, _):
        for number, stage in enumerate((stage0, stage1, stage2, stage3, stage4, stage5)):
            pl.when(s == number)(stage)

        def multiply(t, _):
            k, h = t // 2, lax.rem(t, 2)
            i = jnp.where(s == 0, 0, jnp.where(s == 1, 1, jnp.where(s == 3, 2, k)))
            n = jnp.where(s < 2, 0, jnp.where(s == 2, 1, jnp.where(s == 3, k, s - 2)))
            shift = jnp.where(n == 0, 0, jnp.where(n == 1, 3, jnp.where(n == 2, 1, 2)))
            c = lax.rem(jnp.where(h == 0, x, y) + shift, 4)
            b = lax.rem(n, 2)
            spot = (
                pl.ds(pl.multiple_of(i * WIDE, WIDE), WIDE),
                pl.ds(pl.multiple_of(h * 3 * WIDE, 3 * WIDE), 3 * WIDE),
            )
            acc[spot] += dot3(lh[i, c], ll[i, c], rh[b, h], rl[b, h])
            return 0

        lax.fori_loop(0, 2 * jnp.where(s < 2, 1, jnp.where(s < 4, 2, 3)), multiply, 0)
        return 0

    lax.fori_loop(0, 6, run, 0)

    result = pltpu.make_async_copy(acc, out_ref, osem)
    result.start()
    for make in sent:
        make().wait_send()
    result.wait()


def spread(tile_map, three_centre, occupied, virtual):
    any_space, vmem = pl.BlockSpec(memory_space=pl.ANY), pl.BlockSpec(memory_space=pltpu.VMEM)
    dma = pltpu.SemaphoreType.DMA
    return pl.pallas_call(
        spread_kernel,
        name="spread",
        out_shape=(
            jax.ShapeDtypeStruct((2, 4, 4, HALF_BLOCKS, 8, 128), F32),
            jax.ShapeDtypeStruct((2, 3, PAIRS, WIDE), F32),
            jax.ShapeDtypeStruct((16, 8, 128), jnp.int32),
            jax.ShapeDtypeStruct((8, 8, 128), jnp.int32),
        ),
        in_specs=[any_space] * 4,
        out_specs=(any_space, any_space, vmem, vmem),
        scratch_shapes=[
            pltpu.SMEM((1, 2 * HALF_BLOCKS), jnp.int32),
            pltpu.VMEM((1024, PAIRS), F32),
            pltpu.VMEM((1024, PAIRS), F32),
            pltpu.VMEM((6, 1024, WIDE), F32),
            pltpu.VMEM((2 * PAIRS, 1024), BF16),
            pltpu.VMEM((2 * PAIRS, 1024), BF16),
            pltpu.VMEM((2, HALF_BLOCKS, PAIRS, 128), F32),
            pltpu.VMEM((2, 3, PAIRS, WIDE), F32),
            pltpu.VMEM((2, 4, HALF_BLOCKS, 32, 128), F32),
            pltpu.VMEM((4, 4, 8, 128), jnp.int32),
            pltpu.VMEM((8, 8, 128), jnp.int32),
            pltpu.VMEM((2, 3, PAIRS, WIDE), F32),
            pltpu.VMEM((2, 3, PAIRS, WIDE), F32),
            dma((3,)), dma((6,)), dma((2, 3)), dma((2, 3)), dma((2, 3)), dma((2, 3)), dma((2,)),
            dma((3, 2, 3)), dma((3, 2, 3)),
            dma((2, 3)), dma((2, 3)), dma((7,)), dma((7,)),
        ],
        compiler_params=pltpu.CompilerParams(collective_id=0, has_side_effects=True, vmem_limit_bytes=62 << 20),
    )(tile_map, three_centre, occupied, virtual)


def join(cap, number, table, v2, op):
    any_space = pl.BlockSpec(memory_space=pl.ANY)
    dma = pltpu.SemaphoreType.DMA
    return pl.pallas_call(
        functools.partial(join_kernel, cap),
        name=f"join{cap}",
        out_shape=jax.ShapeDtypeStruct((3 * WIDE, 6 * WIDE), F32),
        in_specs=[any_space] * 3,
        out_specs=any_space,
        scratch_shapes=[pltpu.SMEM((6, TILES), jnp.int32), pltpu.VMEM((2, TILES, 8, 128), F32)]
        + [pltpu.VMEM((4, cap, 8, 128), F32)] * 8
        + [
            pltpu.VMEM((3, 2, 4, 2, PAIRS, WIDE), F32),
            pltpu.VMEM((3, 4, WIDE, 512), BF16),
            pltpu.VMEM((3, 4, WIDE, 512), BF16),
            pltpu.VMEM((2, 2, 512, 3 * WIDE), BF16),
            pltpu.VMEM((2, 2, 512, 3 * WIDE), BF16),
            pltpu.VMEM((3 * WIDE, 6 * WIDE), F32),
            dma((2, 4)), dma((2, 4)), dma((2, 4, 4)), dma((2, 4, 4)),
            dma((3, 4)), dma((3, 4)), dma((3, 4)), dma((3, 4)), dma((3,)), dma, dma((2,)),
        ],
        compiler_params=pltpu.CompilerParams(
            collective_id=number, has_side_effects=True, vmem_limit_bytes=62 << 20
        ),
    )(table, v2, op)


def tables(maps, sums):
    kept = maps[:, 0, : 2 * HALF_BLOCKS].reshape(16, 2, HALF_BLOCKS).transpose(1, 0, 2).reshape(2, TILES)
    order = jnp.arange(TILES, dtype=jnp.int32)
    before = (order[None, :] < order[:, None]).astype(jnp.int32)
    pos = jnp.sum(kept[:, None, :] * before[None], axis=2) * kept
    hit = (pos[:, None, :] == order[None, :, None]) & (kept[:, None, :] == 1)
    idx = jnp.sum(jnp.where(hit, order[None, None, :], 0), axis=2)
    most = jnp.max(jnp.sum(sums[:, 0, : 2 * HALF_BLOCKS].reshape(8, 2, HALF_BLOCKS), axis=2))
    return jnp.concatenate([idx, pos, kept], axis=0), most


def body(three_centre, occupied, virtual, tile_map):
    v2, op, maps, sums = spread(tile_map, three_centre[0], occupied[0], virtual[0])
    table, most = tables(maps, sums)
    branches = [functools.partial(join, cap, i + 1) for i, cap in enumerate(CAPS)]
    chosen = sum((most > cap).astype(jnp.int32) for cap in CAPS[:-1])
    return lax.switch(chosen, branches, table, v2.reshape(2, TILES, 8, 128), op)


def solution(mesh):
    return jax.shard_map(
        body,
        mesh=mesh,
        in_specs=(
            P("row", None, "col"),
            P("row", None, None),
            P("row", None, None),
            P("row", "col"),
        ),
        out_specs=P("row", "col"),
        check_vma=False,
    )
```

```python
import functools

import jax
import jax.numpy as jnp
from jax import lax
from jax.experimental import pallas as pl
from jax.experimental.pallas import tpu as pltpu
from jax.sharding import PartitionSpec as P

MESH = pl.DeviceIdType.MESH
F32, BF16 = jnp.float32, jnp.bfloat16
HALF_BLOCKS = 9
TILES = 16 * HALF_BLOCKS
WIDE = 384
PAIRS = 128
CAPS = (72, 80, 88, 96, TILES)


def place():
    row, col = lax.axis_index("row"), lax.axis_index("col")
    return row // 4, lax.rem(row, 4), col // 2, lax.rem(col, 2)


def device(y, x, z, core):
    return (y * 4 + x, z * 2 + core)


def turn(i, d):
    return lax.rem(i + (d + 4), 4)


def split(x):
    high = x.astype(BF16)
    return high, (x - high.astype(F32)).astype(BF16)


def dot3(ah, al, bh, bl):
    dot = functools.partial(jnp.dot, preferred_element_type=F32)
    return dot(ah, bh) + dot(ah, bl) + dot(al, bh)


def remote(src, dst, send, recv, target):
    return pltpu.make_async_remote_copy(
        src_ref=src, dst_ref=dst, send_sem=send, recv_sem=recv, device_id=target, device_id_type=MESH
    )


def signal(target):
    pl.semaphore_signal(pltpu.get_barrier_semaphore(), inc=1, device_id=target, device_id_type=MESH)


def spread_kernel(
    map_hbm, t_ref, occ_hbm, vir_hbm, v2_ref, op_ref, maps_ref, branch_ref,
    map_ref, occ_ref, vir_ref, tbuf, dh, dl, vbuf, obuf, v1, maps, sums,
    ox, oz, isem, tsem, s1, r1, s2, r2, loc, osend, orecv, ms, mr, ss, sr,
):
    y, x, z, core = place()
    me_row, me_col = y * 4 + x, z * 2 + core
    barrier = pltpu.get_barrier_semaphore()

    loads = [
        pltpu.make_async_copy(t_ref.at[:, pl.ds(i * WIDE, WIDE)], tbuf.at[i], tsem.at[i]) for i in range(6)
    ]
    small = [
        pltpu.make_async_copy(src, dst, isem.at[i])
        for i, (src, dst) in enumerate(((occ_hbm, occ_ref), (vir_hbm, vir_ref), (map_hbm, map_ref)))
    ]
    for load in small + loads:
        load.start()

    for d in (1, 2, 3):
        signal(device(y, turn(x, d), z, core))
        signal(device(turn(y, d), x, z, core))
    for d in range(1, 8):
        signal((me_row, lax.rem(me_col + d, 8)))
    parity = (lax.rem(x, 2), lax.rem(z, 2), lax.rem(y, 2))
    slot = (x // 2, z // 2, y // 2)

    def pair(i):
        return 2 * i + core

    targets = (
        [device(y, 2 * core + i, z, parity[0]) for i in range(2)],
        [device(y, x, pair(i), parity[1]) for i in range(2)],
        [device(pair(i), x, z, parity[2]) for i in range(2)],
    )
    sources = (
        [device(y, pair(i), z, x // 2) for i in range(2)],
        [device(y, x, pair(i), parity[1]) for i in range(2)],
        [device(pair(i), x, z, parity[2]) for i in range(2)],
    )

    def is_me(target):
        return (target[0] == me_row) & (target[1] == me_col)

    for stage in range(3):
        for source in sources[stage]:

            @pl.when(jnp.logical_not(is_me(source)))
            def _():
                signal(source)

    stays = [[is_me(target) for target in line] for line in targets]
    route = (obuf, ox, oz, op_ref)

    def piece(stage, i, q):
        spot = route[stage + 1].at[slot[stage], q]
        recv = orecv.at[stage, slot[stage], q]
        return remote(route[stage].at[i, q], spot, osend.at[stage, i, q], recv, targets[stage][i])

    def piece_start(stage, i, q):
        @pl.when(stays[stage][i])
        def _():
            spot = route[stage + 1].at[slot[stage], q]
            pltpu.make_async_copy(route[stage].at[i, q], spot, orecv.at[stage, slot[stage], q]).start()

        @pl.when(jnp.logical_not(stays[stage][i]))
        def _():
            piece(stage, i, q).start()

    def piece_arrived(stage, i, q):
        spot = route[stage + 1].at[i, q]
        pltpu.make_async_copy(spot, spot, orecv.at[stage, i, q]).wait()

    for part, ref in enumerate((occ_ref, vir_ref)):
        small[part].wait()
        high, low = split(ref[...].T)
        dh[pl.ds(part * PAIRS, PAIRS), :] = high
        dl[pl.ds(part * PAIRS, PAIRS), :] = low

    small[2].wait()
    lane = lax.broadcasted_iota(jnp.int32, (8, 128), 1)
    mine = jnp.zeros((8, 128), jnp.int32)
    for b in range(2 * HALF_BLOCKS):
        mine = jnp.where(lane == b, map_ref[0, b], mine)
    maps[y, x] = mine

    pl.semaphore_wait(barrier, 13 + sum(jnp.where(stay, 0, 1) for line in stays for stay in line))

    told = []
    for d in (1, 2, 3):
        told.append(
            remote(maps.at[y, x], maps.at[y, x], ms.at[0, d - 1], mr.at[0, d - 1], device(y, turn(x, d), z, core))
        )
        told[-1].start()

    first = []
    for h in range(2):
        for q in range(3):
            loads[3 * h + q].wait()

        def chunk(q, _):
            th, tl = split(tbuf[3 * h + q])
            r = dot3(dh[...], dl[...], th, tl)
            for b in range(3):
                keep = map_ref[0, HALF_BLOCKS * h + 3 * q + b].astype(F32)
                cut = slice(b * 128, b * 128 + 128)
                obuf[h, q, :, cut] = r[:PAIRS, cut] * keep
                vbuf[h, 3 * q + b] = r[PAIRS:, cut] * keep
            return 0

        lax.fori_loop(0, 3, chunk, 0)

        if h == 0:
            for copy in told:
                copy.wait_recv()
            for d in (1, 2, 3):
                told.append(
                    remote(maps.at[y], maps.at[y], ms.at[1, d - 1], mr.at[1, d - 1], device(turn(y, d), x, z, core))
                )
                told[-1].start()

        piece_start(0, h, 0)
        here = y if h else x
        sends = []
        for d in (1, 2, 3):
            to = turn(here, d)
            copy = remote(
                vbuf.at[h, :, pl.ds(pl.multiple_of(to * 32, 32), 32), :],
                v1.at[h, here],
                s1.at[h, d - 1],
                r1.at[h, d - 1],
                device(to, x, z, core) if h else device(y, to, z, core),
            )
            copy.start()
            sends.append(copy)
        first.append(sends)
        v1[h, here] = vbuf[h, :, pl.ds(pl.multiple_of(here * 32, 32), 32), :]

    def advance(stage, q):
        for i in range(2):
            piece_arrived(stage, i, q)
            if stage < 2:
                piece_start(stage + 1, i, q)
            if stage == 0 and q < 2:
                piece_start(0, i, q + 1)

    advance(0, 0)
    for copy in told[3:]:
        copy.wait_recv()
    sums[me_col] = jnp.sum(maps[...].reshape(16, 8, 128), axis=0)
    for d in range(1, 8):
        told.append(
            remote(
                sums.at[me_col], sums.at[me_col], ss.at[d - 1], sr.at[d - 1], (me_row, lax.rem(me_col + d, 8))
            )
        )
        told[-1].start()

    second = []
    for h in range(2):
        for copy in first[h]:
            copy.wait_recv()
        here = x if h else y
        spot = v2_ref.at[1, :, x] if h else v2_ref.at[0, y]
        for d in (1, 2, 3):
            to = turn(here, d)
            copy = remote(
                v1.at[h, :, :, pl.ds(pl.multiple_of(to * 8, 8), 8), :],
                spot,
                s2.at[h, d - 1],
                r2.at[h, d - 1],
                device(y, to, z, core) if h else device(to, x, z, core),
            )
            copy.start()
            second.append(copy)
        copy = pltpu.make_async_copy(
            v1.at[h, :, :, pl.ds(pl.multiple_of(here * 8, 8), 8), :], spot, loc.at[h]
        )
        copy.start()
        second.append(copy)
        if h == 0:
            advance(0, 1)
            advance(1, 0)
    advance(0, 2)
    advance(1, 1)
    advance(1, 2)

    for copy in told[6:]:
        copy.wait_recv()
    maps_ref[...] = maps[...].reshape(16, 8, 128)
    counts = sums[...].astype(F32)
    lane = lax.broadcasted_iota(jnp.int32, (8, 8, 128), 2)
    halves = (lane < HALF_BLOCKS, (lane >= HALF_BLOCKS) & (lane < 2 * HALF_BLOCKS))
    most = jnp.maximum(*(jnp.max(jnp.sum(jnp.where(half, counts, 0.0), axis=2)) for half in halves))
    branch_ref[0] = sum((most > cap).astype(jnp.int32) for cap in CAPS[:-1])
    for copy in told:
        copy.wait_send()
    for q in range(3):
        advance(2, q)
    for copy in second:
        copy.wait()
    for h in range(2):
        for copy in first[h]:
            copy.wait_send()
    for stage in range(3):
        for i in range(2):

            @pl.when(jnp.logical_not(stays[stage][i]))
            def _():
                for q in range(3):
                    piece(stage, i, q).wait_send()


def join_kernel(
    cap, table_hbm, v2_hbm, op_ref, acc_out, lh_out, ll_out, rh_out, rl_out, table, v2_ref,
    g00, g01, g02, g03, g10, g11, g12, g13, oall, lh, ll, rh, rl, acc,
    p1s, p1r, p2s, p2r, zs, zr, bs, br, loc, osem, lsem, isem,
):
    y, x, z, core = place()
    small = [pltpu.make_async_copy(table_hbm, table, isem.at[0]), pltpu.make_async_copy(v2_hbm, v2_ref, isem.at[1])]
    for load in small:
        load.start()
    barrier = pltpu.get_barrier_semaphore()
    got = ((g00, g01, g02, g03), (g10, g11, g12, g13))
    near = (
        device(y, turn(x, 1), z, core), device(y, turn(x, -1), z, core),
        device(turn(y, 1), x, z, core), device(turn(y, -1), x, z, core),
        device(y, x, turn(z, 1), core), device(y, x, turn(z, -1), core),
        device(y, x, z, 1 - core),
    )
    for target in near:
        signal(target)
    pl.semaphore_wait(barrier, len(near))
    x_next, x_last, y_next, y_last, z_next, z_last, twin = near
    sent = []

    def go(make):
        make().start()
        sent.append(make)
        return make

    zslot = (z, turn(z, -1), turn(z, 1), turn(z, 2))
    zcopy, bcopy = {}, {}

    def occupied_send(c):
        def first(send, recv, n, target):
            return go(lambda: remote(op_ref.at[:, c], oall.at[c, core, z], send.at[c, n], recv.at[c, n], target))

        zcopy[c, 0] = first(zs, zr, 0, z_next)
        zcopy[c, 1] = first(zs, zr, 1, z_last)
        bcopy[c, 0] = first(bs, br, 0, twin)
        pltpu.make_async_copy(op_ref.at[:, c], oall.at[c, core, z], loc.at[c]).start()

    occupied_send(0)

    def relay(c, n, part, target):
        def make():
            spot = oall.at[c, core, zslot[n], part]
            return remote(spot, spot, zs.at[c, n + 1], zr.at[c, n + 1], target)

        zcopy[c, n + 1] = go(make)

    def share(c, n):
        def make():
            spot = oall.at[c, core, zslot[n]]
            return remote(spot, spot, bs.at[c, n], br.at[c, n], twin)

        bcopy[c, n] = go(make)

    def occupied_near(c):
        for n, target in ((1, z_next), (2, z_last)):
            zcopy[c, n - 1]().wait_recv()
            relay(c, n, n - 1, target)
            share(c, n)

    def occupied_far(c):
        zcopy[c, 2]().wait_recv()
        zcopy[c, 3]().wait_recv()
        share(c, 3)

    def left(c):
        pltpu.make_async_copy(op_ref.at[:, c], oall.at[c, core, z], loc.at[c]).wait()
        for n in range(4):
            bcopy[c, n]().wait_recv()

        def rows(g, _):
            for j in range(4):
                t = oall[c, :, :, :, pl.ds(pl.multiple_of(g * 32, 32) + j * 8, 8), :]
                high, low = split(t.reshape(128, WIDE).T)
                lh[c, g, :, j * 128 : j * 128 + 128] = high
                ll[c, g, :, j * 128 : j * 128 + 128] = low
            return 0

        lax.fori_loop(0, 4, rows, 0)

    around = ((turn(y, -1), turn(y, 1)), (turn(x, -1), turn(x, 1)))
    axes = ((x, y, x_next, x_last, y_next, y_last), (y, x, y_next, y_last, x_next, x_last))
    half_cap = cap // 2
    low_part, high_part = pl.ds(0, half_cap), pl.ds(half_cap, cap - half_cap)
    p1, p2 = {}, {}
    for load in small:
        load.wait()

    parts = (low_part, high_part, high_part, low_part, low_part, high_part)

    def line_move(h, k):
        b, target = axes[h][1], axes[h][2 + k % 2]
        n, there = ((0, 1), (0, 2), (0, 1), (0, 2), (1, 3), (2, 3))[k]

        def make():
            return remote(
                got[h][n].at[b, parts[k]], got[h][there].at[b, parts[k]], p1s.at[h, k], p1r.at[h, k], target
            )

        p1[h, k] = go(make)

    def plane_move(h, n, k):
        target = axes[h][4 + k % 2]
        at = axes[h][1] if k < 4 else around[h][k - 4]

        def make():
            spot = got[h][n].at[at, parts[k]]
            return remote(spot, spot, p2s.at[h, n, k], p2r.at[h, n, k], target)

        p2[h, n, k] = go(make)

    def line_arrived(h, *copies):
        for k in copies:
            p1[h, k]().wait_recv()

    def plane_arrived(h, n, *copies):
        for k in copies:
            p2[h, n, k]().wait_recv()

    for h in range(2):
        b = axes[h][1]

        def pack(i, _):
            for u in range(8):
                got[h][0][b, i * 8 + u] = v2_ref[h, table[h, i * 8 + u]]
            return 0

        lax.fori_loop(0, cap // 8, pack, 0)
        for line in got[h]:
            for j in range(4):
                line[j, cap] = jnp.zeros((8, 128), F32)
        line_move(h, 0)
        line_move(h, 1)
    for h in range(2):
        line_move(h, 2)
        line_move(h, 3)
        plane_move(h, 0, 0)
        plane_move(h, 0, 1)

    both = range(2)

    def early(n):
        for h in both:
            for k in (0, 1):
                if n == 0:
                    line_arrived(h, k)
                    line_move(h, k + 4)
                else:
                    plane_arrived(h, n - 1, k)
                    plane_move(h, n - 1, k + 4)
        if n < 4:
            for h in both:
                plane_move(h, n, 2)
                plane_move(h, n, 3)

    def late(n):
        for h in both:
            if n == 0:
                line_arrived(h, 2, 3)
            else:
                plane_arrived(h, n - 1, 2, 3)
        if n < 3:
            for h in both:
                if n == 2:
                    line_arrived(h, 4, 5)
                plane_move(h, n + 1, 0)
                plane_move(h, n + 1, 1)

    def right(h, n):
        plane_arrived(h, n, 4, 5)

        def columns(q, _):
            for j in range(4):
                tiles = []
                for kk in range(2):
                    for zz in range(4):
                        for i in range(2):
                            m = (2 * i + kk) * 4 + zz
                            t = m * HALF_BLOCKS + q
                            tiles.append(got[h][n][j, jnp.minimum(table[2 + h, t], cap)])
                high, low = split(jnp.concatenate(tiles, axis=0))
                cut = pl.ds(pl.multiple_of(q * 128, 128), 128)
                rh[n % 2, h, j * 128 : j * 128 + 128, cut] = high
                rl[n % 2, h, j * 128 : j * 128 + 128, cut] = low
            return 0

        lax.fori_loop(0, HALF_BLOCKS, columns, 0)

    far = (turn(x, 2), turn(y, 2))
    last_left = [
        functools.partial(lambda h, k, src, dst: pltpu.make_async_copy(src.at[:, far[h]], dst.at[h], lsem.at[h, k]), h, k, src, dst)
        for h in both
        for k, (src, dst) in enumerate(((lh, lh_out), (ll, ll_out)))
    ]
    last_right = [
        functools.partial(lambda k, src, dst: pltpu.make_async_copy(src.at[1], dst, osem.at[3 + k]), k, src, dst)
        for k, (src, dst) in enumerate(((rh, rh_out), (rl, rl_out)))
    ]

    def rows_out(i):
        rows = pl.ds(pl.multiple_of(i * WIDE, WIDE), WIDE)
        return pltpu.make_async_copy(acc.at[rows], acc_out.at[rows], osem.at[i])

    def stage0():
        early(0)
        occupied_near(0)
        occupied_send(1)
        late(0)
        occupied_far(0)
        left(0)
        early(1)
        late(1)
        occupied_near(1)
        occupied_send(2)
        for h in both:
            right(h, 0)

    def stage1():
        early(2)
        occupied_far(1)
        left(1)

    def stage2():
        late(2)
        for h in both:
            right(h, 1)

    def stage3():
        early(3)
        occupied_near(2)

    def stage4():
        late(3)
        occupied_far(2)
        left(2)

    def stage5():
        early(4)
        for copy in last_left:
            copy().start()

    def stage6():
        for h in both:
            right(h, 2)

    def stage7():
        late(4)
        for h in both:
            right(h, 3)
        for copy in last_right:
            copy().start()

    plan = (
        (stage0, 0, 1, 0), (stage1, 1, 1, 0), (stage2, 0, 1, 1), (stage3, 1, 1, 1),
        (stage4, 2, 1, 0), (stage5, 2, 1, 1), (stage6, 0, 3, 2), (stage7, 0, 0, 3),
    )

    def look_up(s, column):
        value = plan[0][column]
        for number, line in enumerate(plan):
            value = jnp.where(s == number, line[column], value)
        return value

    def clear(i, _):
        acc[pl.ds(pl.multiple_of(i * 64, 64), 64), :] = jnp.zeros((64, 6 * WIDE), F32)
        return 0

    lax.fori_loop(0, 18, clear, 0)

    def run(s, _):
        for number, line in enumerate(plan):
            pl.when(s == number)(line[0])
        start, n = look_up(s, 1), look_up(s, 3)
        shift = jnp.where(n == 0, 0, jnp.where(n == 1, 3, jnp.where(n == 2, 1, 2)))

        def multiply(t, _):
            i, h = start + t // 2, lax.rem(t, 2)
            c = lax.rem(jnp.where(h == 0, x, y) + shift, 4)
            b = lax.rem(n, 2)
            spot = (
                pl.ds(pl.multiple_of(i * WIDE, WIDE), WIDE),
                pl.ds(pl.multiple_of(h * 3 * WIDE, 3 * WIDE), 3 * WIDE),
            )
            acc[spot] += dot3(lh[i, c], ll[i, c], rh[b, h], rl[b, h])

            @pl.when((s == 6) & (h == 1))
            def _():
                rows_out(i).start()

            return 0

        lax.fori_loop(0, 2 * look_up(s, 2), multiply, 0)
        return 0

    lax.fori_loop(0, len(plan), run, 0)

    for make in sent:
        make().wait_send()
    for i in range(3):
        rows_out(i).wait()
    for copy in last_left + last_right:
        copy().wait()


def finish_kernel(acc_ref, lh_ref, ll_ref, rh_ref, rl_ref, out_ref):
    out_ref[...] = acc_ref[...] + dot3(lh_ref[0, 0], ll_ref[0, 0], rh_ref[0], rl_ref[0])


def spread(tile_map, three_centre, occupied, virtual):
    any_space, vmem = pl.BlockSpec(memory_space=pl.ANY), pl.BlockSpec(memory_space=pltpu.VMEM)
    dma = pltpu.SemaphoreType.DMA
    return pl.pallas_call(
        spread_kernel,
        name="spread",
        out_shape=(
            jax.ShapeDtypeStruct((2, 4, 4, HALF_BLOCKS, 8, 128), F32),
            jax.ShapeDtypeStruct((2, 3, PAIRS, WIDE), F32),
            jax.ShapeDtypeStruct((16, 8, 128), jnp.int32),
            jax.ShapeDtypeStruct((1,), jnp.int32),
        ),
        in_specs=[any_space] * 4,
        out_specs=(any_space, any_space, vmem, pl.BlockSpec(memory_space=pltpu.SMEM)),
        scratch_shapes=[
            pltpu.SMEM((1, 2 * HALF_BLOCKS), jnp.int32),
            pltpu.VMEM((1024, PAIRS), F32),
            pltpu.VMEM((1024, PAIRS), F32),
            pltpu.VMEM((6, 1024, WIDE), F32),
            pltpu.VMEM((2 * PAIRS, 1024), BF16),
            pltpu.VMEM((2 * PAIRS, 1024), BF16),
            pltpu.VMEM((2, HALF_BLOCKS, PAIRS, 128), F32),
            pltpu.VMEM((2, 3, PAIRS, WIDE), F32),
            pltpu.VMEM((2, 4, HALF_BLOCKS, 32, 128), F32),
            pltpu.VMEM((4, 4, 8, 128), jnp.int32),
            pltpu.VMEM((8, 8, 128), jnp.int32),
            pltpu.VMEM((2, 3, PAIRS, WIDE), F32),
            pltpu.VMEM((2, 3, PAIRS, WIDE), F32),
            dma((3,)), dma((6,)), dma((2, 3)), dma((2, 3)), dma((2, 3)), dma((2, 3)), dma((2,)),
            dma((3, 2, 3)), dma((3, 2, 3)),
            dma((2, 3)), dma((2, 3)), dma((7,)), dma((7,)),
        ],
        compiler_params=pltpu.CompilerParams(collective_id=0, has_side_effects=True, vmem_limit_bytes=62 << 20),
    )(tile_map, three_centre, occupied, virtual)


def join(cap, number, table, v2, op):
    any_space = pl.BlockSpec(memory_space=pl.ANY)
    dma = pltpu.SemaphoreType.DMA
    return pl.pallas_call(
        functools.partial(join_kernel, cap),
        name=f"join{cap}",
        out_shape=(
            jax.ShapeDtypeStruct((3 * WIDE, 6 * WIDE), F32),
            jax.ShapeDtypeStruct((2, 3, WIDE, 512), BF16),
            jax.ShapeDtypeStruct((2, 3, WIDE, 512), BF16),
            jax.ShapeDtypeStruct((2, 512, 3 * WIDE), BF16),
            jax.ShapeDtypeStruct((2, 512, 3 * WIDE), BF16),
        ),
        in_specs=[any_space] * 3,
        out_specs=(any_space,) * 5,
        scratch_shapes=[pltpu.SMEM((4, TILES), jnp.int32), pltpu.VMEM((2, TILES, 8, 128), F32)]
        + [pltpu.VMEM((4, cap + 1, 8, 128), F32)] * 8
        + [
            pltpu.VMEM((3, 2, 4, 2, PAIRS, WIDE), F32),
            pltpu.VMEM((3, 4, WIDE, 512), BF16),
            pltpu.VMEM((3, 4, WIDE, 512), BF16),
            pltpu.VMEM((2, 2, 512, 3 * WIDE), BF16),
            pltpu.VMEM((2, 2, 512, 3 * WIDE), BF16),
            pltpu.VMEM((3 * WIDE, 6 * WIDE), F32),
            dma((2, 6)), dma((2, 6)), dma((2, 4, 6)), dma((2, 4, 6)),
            dma((3, 4)), dma((3, 4)), dma((3, 4)), dma((3, 4)), dma((3,)), dma((5,)), dma((2, 2)), dma((2,)),
        ],
        compiler_params=pltpu.CompilerParams(
            collective_id=number, has_side_effects=True, vmem_limit_bytes=62 << 20
        ),
    )(table, v2, op)


def finish(acc, lh, ll, rh, rl):
    tile = pl.BlockSpec((WIDE, 3 * WIDE), lambda h, i: (i, h))
    left = pl.BlockSpec((1, 1, WIDE, 512), lambda h, i: (h, i, 0, 0))
    right = pl.BlockSpec((1, 512, 3 * WIDE), lambda h, i: (h, 0, 0))
    return pl.pallas_call(
        finish_kernel,
        name="finish",
        grid=(2, 3),
        out_shape=jax.ShapeDtypeStruct((3 * WIDE, 6 * WIDE), F32),
        in_specs=[tile, left, left, right, right],
        out_specs=tile,
        compiler_params=pltpu.CompilerParams(vmem_limit_bytes=40 << 20),
    )(acc, lh, ll, rh, rl)


def tables(maps):
    kept = maps[:, 0, : 2 * HALF_BLOCKS].reshape(16, 2, HALF_BLOCKS).transpose(1, 0, 2).reshape(2, TILES)
    order = jnp.arange(TILES, dtype=jnp.int32)
    before = (order[None, :] < order[:, None]).astype(jnp.int32)
    pos = jnp.where(kept == 1, jnp.sum(kept[:, None, :] * before[None], axis=2), TILES)
    hit = pos[:, None, :] == order[None, :, None]
    idx = jnp.sum(jnp.where(hit, order[None, None, :], 0), axis=2)
    return jnp.concatenate([idx, pos], axis=0)


def body(three_centre, occupied, virtual, tile_map):
    v2, op, maps, chosen = spread(tile_map, three_centre[0], occupied[0], virtual[0])
    table = tables(maps)
    branches = [functools.partial(join, cap, i + 1) for i, cap in enumerate(CAPS)]
    return finish(*lax.switch(chosen[0], branches, table, v2.reshape(2, TILES, 8, 128), op))


def solution(mesh):
    return jax.shard_map(
        body,
        mesh=mesh,
        in_specs=(
            P("row", None, "col"),
            P("row", None, None),
            P("row", None, None),
            P("row", "col"),
        ),
        out_specs=P("row", "col"),
        check_vma=False,
    )
```

```python
import functools

import jax
import jax.numpy as jnp
from jax import lax
from jax.experimental import pallas as pl
from jax.experimental.pallas import tpu as pltpu
from jax.sharding import PartitionSpec as P

MESH = pl.DeviceIdType.MESH
F32, BF16 = jnp.float32, jnp.bfloat16
HALF_BLOCKS = 9
TILES = 16 * HALF_BLOCKS
WIDE = 384
PAIRS = 128
CAPS = (72, 80, 88, 96, TILES)


def place():
    row, col = lax.axis_index("row"), lax.axis_index("col")
    return row // 4, lax.rem(row, 4), col // 2, lax.rem(col, 2)


def device(y, x, z, core):
    return (y * 4 + x, z * 2 + core)


def turn(i, d):
    return lax.rem(i + (d + 4), 4)


def split(x):
    high = x.astype(BF16)
    return high, (x - high.astype(F32)).astype(BF16)


def dot3(ah, al, bh, bl):
    dot = functools.partial(jnp.dot, preferred_element_type=F32)
    return dot(ah, bh) + dot(ah, bl) + dot(al, bh)


def remote(src, dst, send, recv, target):
    return pltpu.make_async_remote_copy(
        src_ref=src, dst_ref=dst, send_sem=send, recv_sem=recv, device_id=target, device_id_type=MESH
    )


def signal(target):
    pl.semaphore_signal(pltpu.get_barrier_semaphore(), inc=1, device_id=target, device_id_type=MESH)


def spread_kernel(
    map_hbm, t_ref, occ_hbm, vir_hbm, v2_ref, op_ref, maps_ref, branch_ref,
    map_ref, occ_ref, vir_ref, tbuf, dh, dl, vbuf, obuf, v1, maps, sums,
    ox, oz, isem, tsem, s1, r1, s2, r2, loc, osend, orecv, ms, mr, ss, sr,
):
    y, x, z, core = place()
    me_row, me_col = y * 4 + x, z * 2 + core
    barrier = pltpu.get_barrier_semaphore()

    loads = [
        pltpu.make_async_copy(t_ref.at[:, pl.ds(i * WIDE, WIDE)], tbuf.at[i], tsem.at[i]) for i in range(6)
    ]
    small = [
        pltpu.make_async_copy(src, dst, isem.at[i])
        for i, (src, dst) in enumerate(((occ_hbm, occ_ref), (vir_hbm, vir_ref), (map_hbm, map_ref)))
    ]
    for load in small + loads:
        load.start()

    for d in (1, 2, 3):
        signal(device(y, turn(x, d), z, core))
        signal(device(turn(y, d), x, z, core))
    for d in range(1, 8):
        signal((me_row, lax.rem(me_col + d, 8)))
    parity = (lax.rem(x, 2), lax.rem(z, 2), lax.rem(y, 2))
    slot = (x // 2, z // 2, y // 2)

    def pair(i):
        return 2 * i + core

    targets = (
        [device(y, 2 * core + i, z, parity[0]) for i in range(2)],
        [device(y, x, pair(i), parity[1]) for i in range(2)],
        [device(pair(i), x, z, parity[2]) for i in range(2)],
    )
    sources = (
        [device(y, pair(i), z, x // 2) for i in range(2)],
        [device(y, x, pair(i), parity[1]) for i in range(2)],
        [device(pair(i), x, z, parity[2]) for i in range(2)],
    )

    def is_me(target):
        return (target[0] == me_row) & (target[1] == me_col)

    for stage in range(3):
        for source in sources[stage]:

            @pl.when(jnp.logical_not(is_me(source)))
            def _():
                signal(source)

    stays = [[is_me(target) for target in line] for line in targets]
    route = (obuf, ox, oz, op_ref)

    def piece(stage, i, q):
        spot = route[stage + 1].at[slot[stage], q]
        recv = orecv.at[stage, slot[stage], q]
        return remote(route[stage].at[i, q], spot, osend.at[stage, i, q], recv, targets[stage][i])

    def piece_start(stage, i, q):
        @pl.when(stays[stage][i])
        def _():
            spot = route[stage + 1].at[slot[stage], q]
            pltpu.make_async_copy(route[stage].at[i, q], spot, orecv.at[stage, slot[stage], q]).start()

        @pl.when(jnp.logical_not(stays[stage][i]))
        def _():
            piece(stage, i, q).start()

    def piece_arrived(stage, i, q):
        spot = route[stage + 1].at[i, q]
        pltpu.make_async_copy(spot, spot, orecv.at[stage, i, q]).wait()

    for part, ref in enumerate((occ_ref, vir_ref)):
        small[part].wait()
        high, low = split(ref[...].T)
        dh[pl.ds(part * PAIRS, PAIRS), :] = high
        dl[pl.ds(part * PAIRS, PAIRS), :] = low

    small[2].wait()
    lane = lax.broadcasted_iota(jnp.int32, (8, 128), 1)
    mine = jnp.zeros((8, 128), jnp.int32)
    for b in range(2 * HALF_BLOCKS):
        mine = jnp.where(lane == b, map_ref[0, b], mine)
    maps[y, x] = mine

    pl.semaphore_wait(barrier, 13 + sum(jnp.where(stay, 0, 1) for line in stays for stay in line))

    told = []
    for d in (1, 2, 3):
        told.append(
            remote(maps.at[y, x], maps.at[y, x], ms.at[0, d - 1], mr.at[0, d - 1], device(y, turn(x, d), z, core))
        )
        told[-1].start()

    first = []
    for h in range(2):
        for q in range(3):
            loads[3 * h + q].wait()

        def chunk(q, _):
            th, tl = split(tbuf[3 * h + q])
            r = dot3(dh[...], dl[...], th, tl)
            for b in range(3):
                keep = map_ref[0, HALF_BLOCKS * h + 3 * q + b].astype(F32)
                cut = slice(b * 128, b * 128 + 128)
                obuf[h, q, :, cut] = r[:PAIRS, cut] * keep
                vbuf[h, 3 * q + b] = r[PAIRS:, cut] * keep
            return 0

        lax.fori_loop(0, 3, chunk, 0)

        if h == 0:
            for copy in told:
                copy.wait_recv()
            for d in (1, 2, 3):
                told.append(
                    remote(maps.at[y], maps.at[y], ms.at[1, d - 1], mr.at[1, d - 1], device(turn(y, d), x, z, core))
                )
                told[-1].start()

        piece_start(0, h, 0)
        here = y if h else x
        sends = []
        for d in (1, 2, 3):
            to = turn(here, d)
            copy = remote(
                vbuf.at[h, :, pl.ds(pl.multiple_of(to * 32, 32), 32), :],
                v1.at[h, here],
                s1.at[h, d - 1],
                r1.at[h, d - 1],
                device(to, x, z, core) if h else device(y, to, z, core),
            )
            copy.start()
            sends.append(copy)
        first.append(sends)
        v1[h, here] = vbuf[h, :, pl.ds(pl.multiple_of(here * 32, 32), 32), :]

    def advance(stage, q):
        for i in range(2):
            piece_arrived(stage, i, q)
            if stage < 2:
                piece_start(stage + 1, i, q)
            if stage == 0 and q < 2:
                piece_start(0, i, q + 1)

    advance(0, 0)
    for copy in told[3:]:
        copy.wait_recv()
    sums[me_col] = jnp.sum(maps[...].reshape(16, 8, 128), axis=0)
    for d in range(1, 8):
        told.append(
            remote(
                sums.at[me_col], sums.at[me_col], ss.at[d - 1], sr.at[d - 1], (me_row, lax.rem(me_col + d, 8))
            )
        )
        told[-1].start()

    second = []
    for h in range(2):
        for copy in first[h]:
            copy.wait_recv()
        here = x if h else y
        spot = v2_ref.at[1, :, x] if h else v2_ref.at[0, y]
        for d in (1, 2, 3):
            to = turn(here, d)
            copy = remote(
                v1.at[h, :, :, pl.ds(pl.multiple_of(to * 8, 8), 8), :],
                spot,
                s2.at[h, d - 1],
                r2.at[h, d - 1],
                device(y, to, z, core) if h else device(to, x, z, core),
            )
            copy.start()
            second.append(copy)
        copy = pltpu.make_async_copy(
            v1.at[h, :, :, pl.ds(pl.multiple_of(here * 8, 8), 8), :], spot, loc.at[h]
        )
        copy.start()
        second.append(copy)
        if h == 0:
            advance(0, 1)
            advance(1, 0)
    advance(0, 2)
    advance(1, 1)
    advance(1, 2)

    for copy in told[6:]:
        copy.wait_recv()
    maps_ref[...] = maps[...].reshape(16, 8, 128)
    counts = sums[...].astype(F32)
    lane = lax.broadcasted_iota(jnp.int32, (8, 8, 128), 2)
    halves = (lane < HALF_BLOCKS, (lane >= HALF_BLOCKS) & (lane < 2 * HALF_BLOCKS))
    most = jnp.maximum(*(jnp.max(jnp.sum(jnp.where(half, counts, 0.0), axis=2)) for half in halves))
    branch_ref[0] = sum((most > cap).astype(jnp.int32) for cap in CAPS[:-1])
    for copy in told:
        copy.wait_send()
    for q in range(3):
        advance(2, q)
    for copy in second:
        copy.wait()
    for h in range(2):
        for copy in first[h]:
            copy.wait_send()
    for stage in range(3):
        for i in range(2):

            @pl.when(jnp.logical_not(stays[stage][i]))
            def _():
                for q in range(3):
                    piece(stage, i, q).wait_send()


def join_kernel(
    cap, table_hbm, v2_hbm, op_ref, acc_out, lh_out, ll_out, rh_out, rl_out, table, v2_ref, *refs
):
    oall, lh, ll, rh, rl, acc, p1s, p1r, p2s, p2r, zs, zr, bs, br, loc, osem, lsem, isem = refs[32:]
    y, x, z, core = place()
    small = [pltpu.make_async_copy(table_hbm, table, isem.at[0]), pltpu.make_async_copy(v2_hbm, v2_ref, isem.at[1])]
    for load in small:
        load.start()
    barrier = pltpu.get_barrier_semaphore()
    got = [[refs[16 * h + 4 * n : 16 * h + 4 * n + 4] for n in range(4)] for h in range(2)]
    near = (
        device(y, turn(x, 1), z, core), device(y, turn(x, -1), z, core),
        device(turn(y, 1), x, z, core), device(turn(y, -1), x, z, core),
        device(y, x, turn(z, 1), core), device(y, x, turn(z, -1), core),
        device(y, x, z, 1 - core),
    )
    for target in near:
        signal(target)
    pl.semaphore_wait(barrier, len(near))
    x_next, x_last, y_next, y_last, z_next, z_last, twin = near
    sent = []

    def go(make):
        make().start()
        sent.append(make)
        return make

    zslot = (z, turn(z, -1), turn(z, 1), turn(z, 2))
    zcopy, bcopy = {}, {}

    def occupied_send(c):
        def first(send, recv, n, target):
            return go(lambda: remote(op_ref.at[:, c], oall.at[c, core, z], send.at[c, n], recv.at[c, n], target))

        zcopy[c, 0] = first(zs, zr, 0, z_next)
        zcopy[c, 1] = first(zs, zr, 1, z_last)
        bcopy[c, 0] = first(bs, br, 0, twin)
        pltpu.make_async_copy(op_ref.at[:, c], oall.at[c, core, z], loc.at[c]).start()

    occupied_send(0)

    def relay(c, n, part, target):
        def make():
            spot = oall.at[c, core, zslot[n], part]
            return remote(spot, spot, zs.at[c, n + 1], zr.at[c, n + 1], target)

        zcopy[c, n + 1] = go(make)

    def share(c, n):
        def make():
            spot = oall.at[c, core, zslot[n]]
            return remote(spot, spot, bs.at[c, n], br.at[c, n], twin)

        bcopy[c, n] = go(make)

    def occupied_near(c):
        for n, target in ((1, z_next), (2, z_last)):
            zcopy[c, n - 1]().wait_recv()
            relay(c, n, n - 1, target)
            share(c, n)

    def occupied_far(c):
        zcopy[c, 2]().wait_recv()
        zcopy[c, 3]().wait_recv()
        share(c, 3)

    def left(c):
        pltpu.make_async_copy(op_ref.at[:, c], oall.at[c, core, z], loc.at[c]).wait()
        for n in range(4):
            bcopy[c, n]().wait_recv()

        def rows(g, _):
            for j in range(4):
                t = oall[c, :, :, :, pl.ds(pl.multiple_of(g * 32, 32) + j * 8, 8), :]
                high, low = split(t.reshape(128, WIDE).T)
                lh[c, g * 4 + j] = high
                ll[c, g * 4 + j] = low
            return 0

        lax.fori_loop(0, 4, rows, 0)

    axes = ((x, y, x_next, x_last, y_next, y_last), (y, x, y_next, y_last, x_next, x_last))
    half_cap = cap // 2
    low_part, high_part = pl.ds(0, half_cap), pl.ds(half_cap, cap - half_cap)
    p1, p2 = {}, {}
    for load in small:
        load.wait()

    parts = (low_part, high_part, high_part, low_part, low_part, high_part)

    def line_move(h, k):
        target = axes[h][2 + k % 2]
        n, there = ((0, 1), (0, 2), (0, 1), (0, 2), (1, 3), (2, 3))[k]

        def make():
            return remote(
                got[h][n][0].at[parts[k]], got[h][there][0].at[parts[k]], p1s.at[h, k], p1r.at[h, k], target
            )

        p1[h, k] = go(make)

    def plane_move(h, n, k):
        target = axes[h][4 + k % 2]
        here, there = ((0, 1), (0, 2), (0, 1), (0, 2), (1, 3), (2, 3))[k]

        def make():
            return remote(
                got[h][n][here].at[parts[k]], got[h][n][there].at[parts[k]], p2s.at[h, n, k], p2r.at[h, n, k], target
            )

        p2[h, n, k] = go(make)

    def line_arrived(h, *copies):
        for k in copies:
            p1[h, k]().wait_recv()

    def plane_arrived(h, n, *copies):
        for k in copies:
            p2[h, n, k]().wait_recv()

    for h in range(2):

        def pack(i, _):
            for u in range(8):
                got[h][0][0][i * 8 + u] = v2_ref[h, table[h, i * 8 + u]]
            return 0

        lax.fori_loop(0, cap // 8, pack, 0)
        for line in got[h]:
            for packed in line:
                packed[cap] = jnp.zeros((8, 128), F32)
        line_move(h, 0)
        line_move(h, 1)
    for h in range(2):
        line_move(h, 2)
        line_move(h, 3)
        plane_move(h, 0, 0)
        plane_move(h, 0, 1)

    both = range(2)

    def early(n):
        for h in both:
            for k in (0, 1):
                if n == 0:
                    line_arrived(h, k)
                    line_move(h, k + 4)
                else:
                    plane_arrived(h, n - 1, k)
                    plane_move(h, n - 1, k + 4)
        if n < 4:
            for h in both:
                plane_move(h, n, 2)
                plane_move(h, n, 3)

    def late(n):
        for h in both:
            if n == 0:
                line_arrived(h, 2, 3)
            else:
                plane_arrived(h, n - 1, 2, 3)
        if n < 3:
            for h in both:
                plane_move(h, n + 1, 0)
                plane_move(h, n + 1, 1)

    groups = (
        ((0, 0), (1, 0), (2, 0), (3, 0)),
        ((0, 1), (0, 2), (1, 1), (1, 2)),
        ((2, 1), (2, 2), (0, 3), (1, 3)),
        ((3, 1), (3, 2), (2, 3), (3, 3)),
    )

    def right(h, g):

        def columns(q, _):
            for j, (n, k) in enumerate(groups[g]):
                tiles = []
                for kk in range(2):
                    for zz in range(4):
                        for i in range(2):
                            m = (2 * i + kk) * 4 + zz
                            t = m * HALF_BLOCKS + q
                            tiles.append(got[h][n][k][jnp.minimum(table[2 + h, t], cap)])
                high, low = split(jnp.concatenate(tiles, axis=0))
                cut = pl.ds(pl.multiple_of(q * 128, 128), 128)
                rh[g % 2, h, j * 128 : j * 128 + 128, cut] = high
                rl[g % 2, h, j * 128 : j * 128 + 128, cut] = low
            return 0

        lax.fori_loop(0, HALF_BLOCKS, columns, 0)

    def shift(k):
        return jnp.where(k == 0, 0, jnp.where(k == 1, 3, jnp.where(k == 2, 1, 2)))

    def left_at(h, n, k):
        first, second = jnp.where(h == 0, x, y), jnp.where(h == 0, y, x)
        return lax.rem(first + shift(n), 4) * 4 + lax.rem(second + shift(k), 4)

    last_at = [[left_at(h, n, k) for n, k in groups[3]] for h in both]

    def last_left():
        return [
            pltpu.make_async_copy(src.at[:, last_at[h][j]], dst.at[h, j], lsem.at[k, h, j])
            for k, (src, dst) in enumerate(((lh, lh_out), (ll, ll_out)))
            for h in both
            for j in range(4)
        ]

    def last_right():
        return [
            pltpu.make_async_copy(src.at[1], dst, osem.at[3 + k])
            for k, (src, dst) in enumerate(((rh, rh_out), (rl, rl_out)))
        ]

    def rows_out(i):
        rows = pl.ds(pl.multiple_of(i * WIDE, WIDE), WIDE)
        return pltpu.make_async_copy(acc.at[rows], acc_out.at[rows], osem.at[i])

    def stage0():
        early(0)
        occupied_near(0)
        occupied_send(1)
        late(0)
        occupied_far(0)
        left(0)
        for h in both:
            line_arrived(h, 4, 5)
            right(h, 0)

    def stage1():
        early(1)
        occupied_near(1)
        occupied_send(2)
        late(1)
        occupied_far(1)
        left(1)

    def stage2():
        early(2)
        late(2)
        for h in both:
            right(h, 1)

    def stage3():
        early(3)
        occupied_near(2)

    def stage4():
        late(3)
        occupied_far(2)
        left(2)
        for copy in last_left():
            copy.start()

    def stage5():
        early(4)
        for h in both:
            plane_arrived(h, 0, 4, 5)
            plane_arrived(h, 1, 4, 5)

    def stage6():
        for h in both:
            right(h, 2)

    def stage7():
        late(4)
        for h in both:
            plane_arrived(h, 2, 4, 5)
            plane_arrived(h, 3, 4, 5)
            right(h, 3)
        for copy in last_right():
            copy.start()

    plan = (
        (stage0, 0, 1, 0), (stage1, 1, 1, 0), (stage2, 0, 1, 1), (stage3, 1, 1, 1),
        (stage4, 2, 1, 0), (stage5, 2, 1, 1), (stage6, 0, 3, 2), (stage7, 0, 0, 3),
    )

    def look_up(s, column):
        value = plan[0][column]
        for number, line in enumerate(plan):
            value = jnp.where(s == number, line[column], value)
        return value

    def clear(i, _):
        acc[pl.ds(pl.multiple_of(i * 64, 64), 64), :] = jnp.zeros((64, 6 * WIDE), F32)
        return 0

    lax.fori_loop(0, 18, clear, 0)

    def run(s, _):
        for number, line in enumerate(plan):
            pl.when(s == number)(line[0])
        start, g = look_up(s, 1), look_up(s, 3)
        places = []
        for j in range(4):
            n, k = groups[0][j]
            for number in (1, 2):
                n = jnp.where(g == number, groups[number][j][0], n)
                k = jnp.where(g == number, groups[number][j][1], k)
            places.append((n, k))

        def multiply(t, _):
            i, h = start + t // 2, lax.rem(t, 2)
            rows = [left_at(h, n, k) for n, k in places]
            b = lax.rem(g, 2)
            spot = (
                pl.ds(pl.multiple_of(i * WIDE, WIDE), WIDE),
                pl.ds(pl.multiple_of(h * 3 * WIDE, 3 * WIDE), 3 * WIDE),
            )
            high, low = (jnp.concatenate([ref[i, r] for r in rows], axis=1) for ref in (lh, ll))
            acc[spot] += dot3(high, low, rh[b, h], rl[b, h])

            @pl.when((s == 6) & (h == 1))
            def _():
                rows_out(i).start()

            return 0

        lax.fori_loop(0, 2 * look_up(s, 2), multiply, 0)
        return 0

    lax.fori_loop(0, len(plan), run, 0)

    for make in sent:
        make().wait_send()
    for i in range(3):
        rows_out(i).wait()
    for copy in last_left() + last_right():
        copy.wait()


def finish_kernel(acc_ref, lh_ref, ll_ref, rh_ref, rl_ref, out_ref):
    high, low = (jnp.concatenate([ref[0, j, 0] for j in range(4)], axis=1) for ref in (lh_ref, ll_ref))
    out_ref[...] = acc_ref[...] + dot3(high, low, rh_ref[0], rl_ref[0])


def spread(tile_map, three_centre, occupied, virtual):
    any_space, vmem = pl.BlockSpec(memory_space=pl.ANY), pl.BlockSpec(memory_space=pltpu.VMEM)
    dma = pltpu.SemaphoreType.DMA
    return pl.pallas_call(
        spread_kernel,
        name="spread",
        out_shape=(
            jax.ShapeDtypeStruct((2, 4, 4, HALF_BLOCKS, 8, 128), F32),
            jax.ShapeDtypeStruct((2, 3, PAIRS, WIDE), F32),
            jax.ShapeDtypeStruct((16, 8, 128), jnp.int32),
            jax.ShapeDtypeStruct((1,), jnp.int32),
        ),
        in_specs=[any_space] * 4,
        out_specs=(any_space, any_space, vmem, pl.BlockSpec(memory_space=pltpu.SMEM)),
        scratch_shapes=[
            pltpu.SMEM((1, 2 * HALF_BLOCKS), jnp.int32),
            pltpu.VMEM((1024, PAIRS), F32),
            pltpu.VMEM((1024, PAIRS), F32),
            pltpu.VMEM((6, 1024, WIDE), F32),
            pltpu.VMEM((2 * PAIRS, 1024), BF16),
            pltpu.VMEM((2 * PAIRS, 1024), BF16),
            pltpu.VMEM((2, HALF_BLOCKS, PAIRS, 128), F32),
            pltpu.VMEM((2, 3, PAIRS, WIDE), F32),
            pltpu.VMEM((2, 4, HALF_BLOCKS, 32, 128), F32),
            pltpu.VMEM((4, 4, 8, 128), jnp.int32),
            pltpu.VMEM((8, 8, 128), jnp.int32),
            pltpu.VMEM((2, 3, PAIRS, WIDE), F32),
            pltpu.VMEM((2, 3, PAIRS, WIDE), F32),
            dma((3,)), dma((6,)), dma((2, 3)), dma((2, 3)), dma((2, 3)), dma((2, 3)), dma((2,)),
            dma((3, 2, 3)), dma((3, 2, 3)),
            dma((2, 3)), dma((2, 3)), dma((7,)), dma((7,)),
        ],
        compiler_params=pltpu.CompilerParams(collective_id=0, has_side_effects=True, vmem_limit_bytes=62 << 20),
    )(tile_map, three_centre, occupied, virtual)


def join(cap, number, table, v2, op):
    any_space = pl.BlockSpec(memory_space=pl.ANY)
    dma = pltpu.SemaphoreType.DMA
    return pl.pallas_call(
        functools.partial(join_kernel, cap),
        name=f"join{cap}",
        out_shape=(
            jax.ShapeDtypeStruct((3 * WIDE, 6 * WIDE), F32),
            jax.ShapeDtypeStruct((2, 4, 3, WIDE, 128), BF16),
            jax.ShapeDtypeStruct((2, 4, 3, WIDE, 128), BF16),
            jax.ShapeDtypeStruct((2, 512, 3 * WIDE), BF16),
            jax.ShapeDtypeStruct((2, 512, 3 * WIDE), BF16),
        ),
        in_specs=[any_space] * 3,
        out_specs=(any_space,) * 5,
        scratch_shapes=[pltpu.SMEM((4, TILES), jnp.int32), pltpu.VMEM((2, TILES, 8, 128), F32)]
        + [pltpu.VMEM((cap + 1, 8, 128), F32)] * 32
        + [
            pltpu.VMEM((3, 2, 4, 2, PAIRS, WIDE), F32),
            pltpu.VMEM((3, 16, WIDE, 128), BF16),
            pltpu.VMEM((3, 16, WIDE, 128), BF16),
            pltpu.VMEM((2, 2, 512, 3 * WIDE), BF16),
            pltpu.VMEM((2, 2, 512, 3 * WIDE), BF16),
            pltpu.VMEM((3 * WIDE, 6 * WIDE), F32),
            dma((2, 6)), dma((2, 6)), dma((2, 4, 6)), dma((2, 4, 6)),
            dma((3, 4)), dma((3, 4)), dma((3, 4)), dma((3, 4)), dma((3,)), dma((5,)), dma((2, 2, 4)), dma((2,)),
        ],
        compiler_params=pltpu.CompilerParams(
            collective_id=number, has_side_effects=True, vmem_limit_bytes=62 << 20
        ),
    )(table, v2, op)


def finish(acc, lh, ll, rh, rl):
    tile = pl.BlockSpec((WIDE, 3 * WIDE), lambda h, i: (i, h))
    left = pl.BlockSpec((1, 4, 1, WIDE, 128), lambda h, i: (h, 0, i, 0, 0))
    right = pl.BlockSpec((1, 512, 3 * WIDE), lambda h, i: (h, 0, 0))
    return pl.pallas_call(
        finish_kernel,
        name="finish",
        grid=(2, 3),
        out_shape=jax.ShapeDtypeStruct((3 * WIDE, 6 * WIDE), F32),
        in_specs=[tile, left, left, right, right],
        out_specs=tile,
        compiler_params=pltpu.CompilerParams(vmem_limit_bytes=40 << 20),
    )(acc, lh, ll, rh, rl)


def tables(maps):
    kept = maps[:, 0, : 2 * HALF_BLOCKS].reshape(16, 2, HALF_BLOCKS).transpose(1, 0, 2).reshape(2, TILES)
    order = jnp.arange(TILES, dtype=jnp.int32)
    before = (order[None, :] < order[:, None]).astype(jnp.int32)
    pos = jnp.where(kept == 1, jnp.sum(kept[:, None, :] * before[None], axis=2), TILES)
    hit = pos[:, None, :] == order[None, :, None]
    idx = jnp.sum(jnp.where(hit, order[None, None, :], 0), axis=2)
    return jnp.concatenate([idx, pos], axis=0)


def body(three_centre, occupied, virtual, tile_map):
    v2, op, maps, chosen = spread(tile_map, three_centre[0], occupied[0], virtual[0])
    table = tables(maps)
    branches = [functools.partial(join, cap, i + 1) for i, cap in enumerate(CAPS)]
    return finish(*lax.switch(chosen[0], branches, table, v2.reshape(2, TILES, 8, 128), op))


def solution(mesh):
    return jax.shard_map(
        body,
        mesh=mesh,
        in_specs=(
            P("row", None, "col"),
            P("row", None, None),
            P("row", None, None),
            P("row", "col"),
        ),
        out_specs=P("row", "col"),
        check_vma=False,
    )
```

```python
import functools

import jax
import jax.numpy as jnp
from jax import lax
from jax.experimental import pallas as pl
from jax.experimental.pallas import tpu as pltpu
from jax.sharding import PartitionSpec as P

MESH = pl.DeviceIdType.MESH
F32, BF16 = jnp.float32, jnp.bfloat16
HALF_BLOCKS = 9
TILES = 16 * HALF_BLOCKS
WIDE = 384
PAIRS = 128
CAPS = (72, 76, 80, 84, 88, 96, TILES)


def place():
    row, col = lax.axis_index("row"), lax.axis_index("col")
    return row // 4, lax.rem(row, 4), col // 2, lax.rem(col, 2)


def device(y, x, z, core):
    return (y * 4 + x, z * 2 + core)


def turn(i, d):
    return lax.rem(i + (d + 4), 4)


def split(x):
    high = x.astype(BF16)
    return high, (x - high.astype(F32)).astype(BF16)


def dot3(ah, al, bh, bl):
    dot = functools.partial(jnp.dot, preferred_element_type=F32)
    return dot(ah, bh) + dot(ah, bl) + dot(al, bh)


def remote(src, dst, send, recv, target):
    return pltpu.make_async_remote_copy(
        src_ref=src, dst_ref=dst, send_sem=send, recv_sem=recv, device_id=target, device_id_type=MESH
    )


def signal(target):
    pl.semaphore_signal(pltpu.get_barrier_semaphore(), inc=1, device_id=target, device_id_type=MESH)


def spread_kernel(
    map_hbm, t_ref, occ_hbm, vir_hbm, v2_ref, op_ref, maps_ref, branch_ref,
    map_ref, occ_ref, vir_ref, tbuf, dh, dl, vbuf, obuf, v1, maps, sums,
    ox, oz, isem, tsem, s1, r1, s2, r2, loc, osend, orecv, ms, mr, ss, sr,
):
    y, x, z, core = place()
    me_row, me_col = y * 4 + x, z * 2 + core
    barrier = pltpu.get_barrier_semaphore()

    loads = [
        pltpu.make_async_copy(t_ref.at[:, pl.ds(i * WIDE, WIDE)], tbuf.at[i], tsem.at[i]) for i in range(6)
    ]
    small = [
        pltpu.make_async_copy(src, dst, isem.at[i])
        for i, (src, dst) in enumerate(((occ_hbm, occ_ref), (vir_hbm, vir_ref), (map_hbm, map_ref)))
    ]
    for load in small + loads:
        load.start()

    for d in (1, 2, 3):
        signal(device(y, turn(x, d), z, core))
        signal(device(turn(y, d), x, z, core))
    for d in range(1, 8):
        signal((me_row, lax.rem(me_col + d, 8)))
    parity = (lax.rem(x, 2), lax.rem(z, 2), lax.rem(y, 2))
    slot = (x // 2, z // 2, y // 2)

    def pair(i):
        return 2 * i + core

    targets = (
        [device(y, 2 * core + i, z, parity[0]) for i in range(2)],
        [device(y, x, pair(i), parity[1]) for i in range(2)],
        [device(pair(i), x, z, parity[2]) for i in range(2)],
    )
    sources = (
        [device(y, pair(i), z, x // 2) for i in range(2)],
        [device(y, x, pair(i), parity[1]) for i in range(2)],
        [device(pair(i), x, z, parity[2]) for i in range(2)],
    )

    def is_me(target):
        return (target[0] == me_row) & (target[1] == me_col)

    for stage in range(3):
        for source in sources[stage]:

            @pl.when(jnp.logical_not(is_me(source)))
            def _():
                signal(source)

    stays = [[is_me(target) for target in line] for line in targets]
    route = (obuf, ox, oz, op_ref)

    def piece(stage, i, q):
        spot = route[stage + 1].at[slot[stage], q]
        recv = orecv.at[stage, slot[stage], q]
        return remote(route[stage].at[i, q], spot, osend.at[stage, i, q], recv, targets[stage][i])

    def piece_start(stage, i, q):
        @pl.when(stays[stage][i])
        def _():
            spot = route[stage + 1].at[slot[stage], q]
            pltpu.make_async_copy(route[stage].at[i, q], spot, orecv.at[stage, slot[stage], q]).start()

        @pl.when(jnp.logical_not(stays[stage][i]))
        def _():
            piece(stage, i, q).start()

    def piece_arrived(stage, i, q):
        spot = route[stage + 1].at[i, q]
        pltpu.make_async_copy(spot, spot, orecv.at[stage, i, q]).wait()

    for part, ref in enumerate((occ_ref, vir_ref)):
        small[part].wait()
        high, low = split(ref[...].T)
        dh[pl.ds(part * PAIRS, PAIRS), :] = high
        dl[pl.ds(part * PAIRS, PAIRS), :] = low

    small[2].wait()
    lane = lax.broadcasted_iota(jnp.int32, (8, 128), 1)
    mine = jnp.zeros((8, 128), jnp.int32)
    for b in range(2 * HALF_BLOCKS):
        mine = jnp.where(lane == b, map_ref[0, b], mine)
    maps[y, x] = mine

    pl.semaphore_wait(barrier, 13 + sum(jnp.where(stay, 0, 1) for line in stays for stay in line))

    told = []
    for d in (1, 2, 3):
        told.append(
            remote(maps.at[y, x], maps.at[y, x], ms.at[0, d - 1], mr.at[0, d - 1], device(y, turn(x, d), z, core))
        )
        told[-1].start()

    first = []
    for h in range(2):
        for q in range(3):
            loads[3 * h + q].wait()

        def chunk(q, _):
            th, tl = split(tbuf[3 * h + q])
            r = dot3(dh[...], dl[...], th, tl)
            for b in range(3):
                keep = map_ref[0, HALF_BLOCKS * h + 3 * q + b].astype(F32)
                cut = slice(b * 128, b * 128 + 128)
                obuf[h, q, :, cut] = r[:PAIRS, cut] * keep
                vbuf[h, 3 * q + b] = r[PAIRS:, cut] * keep
            return 0

        lax.fori_loop(0, 3, chunk, 0)

        if h == 0:
            for copy in told:
                copy.wait_recv()
            for d in (1, 2, 3):
                told.append(
                    remote(maps.at[y], maps.at[y], ms.at[1, d - 1], mr.at[1, d - 1], device(turn(y, d), x, z, core))
                )
                told[-1].start()

        piece_start(0, h, 0)
        piece_start(0, h, 1)
        here = y if h else x
        sends = []
        for d in (1, 2, 3):
            to = turn(here, d)
            copy = remote(
                vbuf.at[h, :, pl.ds(pl.multiple_of(to * 32, 32), 32), :],
                v1.at[h, here],
                s1.at[h, d - 1],
                r1.at[h, d - 1],
                device(to, x, z, core) if h else device(y, to, z, core),
            )
            copy.start()
            sends.append(copy)
        first.append(sends)
        v1[h, here] = vbuf[h, :, pl.ds(pl.multiple_of(here * 32, 32), 32), :]

    def advance(stage, q):
        for i in range(2):
            piece_arrived(stage, i, q)
            if stage < 2:
                piece_start(stage + 1, i, q)
            if stage == 0 and q == 0:
                piece_start(0, i, 2)

    advance(0, 0)
    for copy in told[3:]:
        copy.wait_recv()
    sums[me_col] = jnp.sum(maps[...].reshape(16, 8, 128), axis=0)
    for d in range(1, 8):
        told.append(
            remote(
                sums.at[me_col], sums.at[me_col], ss.at[d - 1], sr.at[d - 1], (me_row, lax.rem(me_col + d, 8))
            )
        )
        told[-1].start()

    second = []
    for h in range(2):
        for copy in first[h]:
            copy.wait_recv()
        here = x if h else y
        spot = v2_ref.at[1, :, x] if h else v2_ref.at[0, y]
        for d in (1, 2, 3):
            to = turn(here, d)
            copy = remote(
                v1.at[h, :, :, pl.ds(pl.multiple_of(to * 8, 8), 8), :],
                spot,
                s2.at[h, d - 1],
                r2.at[h, d - 1],
                device(y, to, z, core) if h else device(to, x, z, core),
            )
            copy.start()
            second.append(copy)
        copy = pltpu.make_async_copy(
            v1.at[h, :, :, pl.ds(pl.multiple_of(here * 8, 8), 8), :], spot, loc.at[h]
        )
        copy.start()
        second.append(copy)
        if h == 0:
            advance(0, 1)
            advance(1, 0)
    advance(0, 2)
    advance(1, 1)
    advance(1, 2)

    for copy in told[6:]:
        copy.wait_recv()
    maps_ref[...] = maps[...].reshape(16, 8, 128)
    counts = sums[...].astype(F32)
    lane = lax.broadcasted_iota(jnp.int32, (8, 8, 128), 2)
    halves = (lane < HALF_BLOCKS, (lane >= HALF_BLOCKS) & (lane < 2 * HALF_BLOCKS))
    most = jnp.maximum(*(jnp.max(jnp.sum(jnp.where(half, counts, 0.0), axis=2)) for half in halves))
    branch_ref[0] = sum((most > cap).astype(jnp.int32) for cap in CAPS[:-1])
    for copy in told:
        copy.wait_send()
    for q in range(3):
        advance(2, q)
    for copy in second:
        copy.wait()
    for h in range(2):
        for copy in first[h]:
            copy.wait_send()
    for stage in range(3):
        for i in range(2):

            @pl.when(jnp.logical_not(stays[stage][i]))
            def _():
                for q in range(3):
                    piece(stage, i, q).wait_send()


def join_kernel(
    cap, table_hbm, v2_hbm, op_ref, acc_out, lh_out, ll_out, rh_out, rl_out, table, v2_ref, *refs
):
    oall, lh, ll, rh, rl, acc, p1s, p1r, p2s, p2r, zs, zr, bs, br, loc, osem, lsem, isem = refs[32:]
    y, x, z, core = place()
    small = [pltpu.make_async_copy(table_hbm, table, isem.at[0]), pltpu.make_async_copy(v2_hbm, v2_ref, isem.at[1])]
    for load in small:
        load.start()
    barrier = pltpu.get_barrier_semaphore()
    got = [[refs[16 * h + 4 * n : 16 * h + 4 * n + 4] for n in range(4)] for h in range(2)]
    near = (
        device(y, turn(x, 1), z, core), device(y, turn(x, -1), z, core),
        device(turn(y, 1), x, z, core), device(turn(y, -1), x, z, core),
        device(y, x, turn(z, 1), core), device(y, x, turn(z, -1), core),
        device(y, x, z, 1 - core),
    )
    for target in near:
        signal(target)
    pl.semaphore_wait(barrier, len(near))
    x_next, x_last, y_next, y_last, z_next, z_last, twin = near
    sent = []

    def go(make):
        make().start()
        sent.append(make)
        return make

    zslot = (z, turn(z, -1), turn(z, 1), turn(z, 2))
    zcopy, bcopy = {}, {}

    def occupied_send(c):
        def first(send, recv, n, target):
            return go(lambda: remote(op_ref.at[:, c], oall.at[c, core, z], send.at[c, n], recv.at[c, n], target))

        zcopy[c, 0] = first(zs, zr, 0, z_next)
        zcopy[c, 1] = first(zs, zr, 1, z_last)
        bcopy[c, 0] = first(bs, br, 0, twin)
        pltpu.make_async_copy(op_ref.at[:, c], oall.at[c, core, z], loc.at[c]).start()

    occupied_send(0)

    def relay(c, n, part, target):
        def make():
            spot = oall.at[c, core, zslot[n], part]
            return remote(spot, spot, zs.at[c, n + 1], zr.at[c, n + 1], target)

        zcopy[c, n + 1] = go(make)

    def share(c, n):
        def make():
            spot = oall.at[c, core, zslot[n]]
            return remote(spot, spot, bs.at[c, n], br.at[c, n], twin)

        bcopy[c, n] = go(make)

    def occupied_near(c):
        for n, target in ((1, z_next), (2, z_last)):
            zcopy[c, n - 1]().wait_recv()
            relay(c, n, n - 1, target)
            share(c, n)

    def occupied_far(c):
        zcopy[c, 2]().wait_recv()
        zcopy[c, 3]().wait_recv()
        share(c, 3)

    def left(c):
        pltpu.make_async_copy(op_ref.at[:, c], oall.at[c, core, z], loc.at[c]).wait()
        for n in range(4):
            bcopy[c, n]().wait_recv()

        def rows(g, _):
            for j in range(4):
                t = oall[c, :, :, :, pl.ds(pl.multiple_of(g * 32, 32) + j * 8, 8), :]
                high, low = split(t.reshape(128, WIDE).T)
                lh[c, g * 4 + j] = high
                ll[c, g * 4 + j] = low
            return 0

        lax.fori_loop(0, 4, rows, 0)

    axes = ((x, y, x_next, x_last, y_next, y_last), (y, x, y_next, y_last, x_next, x_last))
    half_cap = cap // 2
    low_part, high_part = pl.ds(0, half_cap), pl.ds(half_cap, cap - half_cap)
    p1, p2 = {}, {}
    for load in small:
        load.wait()

    parts = (low_part, high_part, high_part, low_part, low_part, high_part)

    def line_move(h, k):
        target = axes[h][2 + k % 2]
        n, there = ((0, 1), (0, 2), (0, 1), (0, 2), (1, 3), (2, 3))[k]

        def make():
            return remote(
                got[h][n][0].at[parts[k]], got[h][there][0].at[parts[k]], p1s.at[h, k], p1r.at[h, k], target
            )

        p1[h, k] = go(make)

    def plane_move(h, n, k):
        target = axes[h][4 + k % 2]
        here, there = ((0, 1), (0, 2), (0, 1), (0, 2), (1, 3), (2, 3))[k]

        def make():
            return remote(
                got[h][n][here].at[parts[k]], got[h][n][there].at[parts[k]], p2s.at[h, n, k], p2r.at[h, n, k], target
            )

        p2[h, n, k] = go(make)

    def line_arrived(h, *copies):
        for k in copies:
            p1[h, k]().wait_recv()

    def plane_arrived(h, n, *copies):
        for k in copies:
            p2[h, n, k]().wait_recv()

    for h in range(2):

        def pack(i, _):
            for u in range(4):
                got[h][0][0][i * 4 + u] = v2_ref[h, table[h, i * 4 + u]]
            return 0

        lax.fori_loop(0, cap // 4, pack, 0)
        for line in got[h]:
            for packed in line:
                packed[cap] = jnp.zeros((8, 128), F32)
        line_move(h, 0)
        line_move(h, 1)
    for h in range(2):
        line_move(h, 2)
        line_move(h, 3)
        plane_move(h, 0, 0)
        plane_move(h, 0, 1)

    both = range(2)

    def early(n):
        for h in both:
            for k in (0, 1):
                if n == 0:
                    line_arrived(h, k)
                    line_move(h, k + 4)
                else:
                    plane_arrived(h, n - 1, k)
                    plane_move(h, n - 1, k + 4)
        if n < 4:
            for h in both:
                plane_move(h, n, 2)
                plane_move(h, n, 3)

    def late(n):
        for h in both:
            if n == 0:
                line_arrived(h, 2, 3)
            else:
                plane_arrived(h, n - 1, 2, 3)
        if n < 3:
            for h in both:
                plane_move(h, n + 1, 0)
                plane_move(h, n + 1, 1)

    groups = (
        ((0, 0), (1, 0), (2, 0), (3, 0)),
        ((0, 1), (0, 2), (1, 1), (1, 2)),
        ((2, 1), (2, 2), (0, 3), (1, 3)),
        ((3, 1), (3, 2), (2, 3), (3, 3)),
    )

    def right(h, g):

        def columns(q, _):
            for j, (n, k) in enumerate(groups[g]):
                tiles = []
                for kk in range(2):
                    for zz in range(4):
                        for i in range(2):
                            m = (2 * i + kk) * 4 + zz
                            t = m * HALF_BLOCKS + q
                            tiles.append(got[h][n][k][jnp.minimum(table[2 + h, t], cap)])
                high, low = split(jnp.concatenate(tiles, axis=0))
                cut = pl.ds(pl.multiple_of(q * 128, 128), 128)
                rh[g % 2, h, j * 128 : j * 128 + 128, cut] = high
                rl[g % 2, h, j * 128 : j * 128 + 128, cut] = low
            return 0

        lax.fori_loop(0, HALF_BLOCKS, columns, 0)

    def shift(k):
        return jnp.where(k == 0, 0, jnp.where(k == 1, 3, jnp.where(k == 2, 1, 2)))

    def left_at(h, n, k):
        first, second = jnp.where(h == 0, x, y), jnp.where(h == 0, y, x)
        return lax.rem(first + shift(n), 4) * 4 + lax.rem(second + shift(k), 4)

    last_at = [[left_at(h, n, k) for n, k in groups[3]] for h in both]

    def last_left():
        return [
            pltpu.make_async_copy(src.at[:, last_at[h][j]], dst.at[h, j], lsem.at[k, h, j])
            for k, (src, dst) in enumerate(((lh, lh_out), (ll, ll_out)))
            for h in both
            for j in range(4)
        ]

    def last_right():
        return [
            pltpu.make_async_copy(src.at[1], dst, osem.at[3 + k])
            for k, (src, dst) in enumerate(((rh, rh_out), (rl, rl_out)))
        ]

    def rows_out(i):
        rows = pl.ds(pl.multiple_of(i * WIDE, WIDE), WIDE)
        return pltpu.make_async_copy(acc.at[rows], acc_out.at[rows], osem.at[i])

    def stage0():
        early(0)
        occupied_near(0)
        occupied_send(1)
        late(0)
        occupied_far(0)
        left(0)
        for h in both:
            line_arrived(h, 4, 5)
            right(h, 0)

    def stage1():
        early(1)
        occupied_near(1)
        occupied_send(2)
        late(1)
        occupied_far(1)
        left(1)

    def stage2():
        early(2)
        late(2)
        for h in both:
            right(h, 1)

    def stage3():
        early(3)
        occupied_near(2)

    def stage4():
        late(3)
        occupied_far(2)
        left(2)
        for copy in last_left():
            copy.start()

    def stage5():
        early(4)
        for h in both:
            plane_arrived(h, 0, 4, 5)
            plane_arrived(h, 1, 4, 5)

    def stage6():
        for h in both:
            right(h, 2)

    def stage7():
        late(4)
        for h in both:
            plane_arrived(h, 2, 4, 5)
            plane_arrived(h, 3, 4, 5)
            right(h, 3)
        for copy in last_right():
            copy.start()

    plan = (
        (stage0, 0, 1, 0), (stage1, 1, 1, 0), (stage2, 0, 1, 1), (stage3, 1, 1, 1),
        (stage4, 2, 1, 0), (stage5, 2, 1, 1), (stage6, 0, 3, 2), (stage7, 0, 0, 3),
    )

    def look_up(s, column):
        value = plan[0][column]
        for number, line in enumerate(plan):
            value = jnp.where(s == number, line[column], value)
        return value

    def clear(i, _):
        acc[pl.ds(pl.multiple_of(i * 64, 64), 64), :] = jnp.zeros((64, 6 * WIDE), F32)
        return 0

    lax.fori_loop(0, 18, clear, 0)

    def run(s, _):
        for number, line in enumerate(plan):
            pl.when(s == number)(line[0])
        start, g = look_up(s, 1), look_up(s, 3)
        places = []
        for j in range(4):
            n, k = groups[0][j]
            for number in (1, 2):
                n = jnp.where(g == number, groups[number][j][0], n)
                k = jnp.where(g == number, groups[number][j][1], k)
            places.append((n, k))

        def multiply(t, _):
            i, h = start + t // 2, lax.rem(t, 2)
            rows = [left_at(h, n, k) for n, k in places]
            b = lax.rem(g, 2)
            spot = (
                pl.ds(pl.multiple_of(i * WIDE, WIDE), WIDE),
                pl.ds(pl.multiple_of(h * 3 * WIDE, 3 * WIDE), 3 * WIDE),
            )
            high, low = (jnp.concatenate([ref[i, r] for r in rows], axis=1) for ref in (lh, ll))
            acc[spot] += dot3(high, low, rh[b, h], rl[b, h])

            @pl.when((s == 6) & (h == 1))
            def _():
                rows_out(i).start()

            return 0

        lax.fori_loop(0, 2 * look_up(s, 2), multiply, 0)
        return 0

    lax.fori_loop(0, len(plan), run, 0)

    for make in sent:
        make().wait_send()
    for i in range(3):
        rows_out(i).wait()
    for copy in last_left() + last_right():
        copy.wait()


def finish_kernel(acc_ref, lh_ref, ll_ref, rh_ref, rl_ref, out_ref):
    high, low = (jnp.concatenate([ref[0, j, 0] for j in range(4)], axis=1) for ref in (lh_ref, ll_ref))
    out_ref[...] = acc_ref[...] + dot3(high, low, rh_ref[0], rl_ref[0])


def spread(tile_map, three_centre, occupied, virtual):
    any_space, vmem = pl.BlockSpec(memory_space=pl.ANY), pl.BlockSpec(memory_space=pltpu.VMEM)
    dma = pltpu.SemaphoreType.DMA
    return pl.pallas_call(
        spread_kernel,
        name="spread",
        out_shape=(
            jax.ShapeDtypeStruct((2, 4, 4, HALF_BLOCKS, 8, 128), F32),
            jax.ShapeDtypeStruct((2, 3, PAIRS, WIDE), F32),
            jax.ShapeDtypeStruct((16, 8, 128), jnp.int32),
            jax.ShapeDtypeStruct((1,), jnp.int32),
        ),
        in_specs=[any_space] * 4,
        out_specs=(any_space, any_space, vmem, pl.BlockSpec(memory_space=pltpu.SMEM)),
        scratch_shapes=[
            pltpu.SMEM((1, 2 * HALF_BLOCKS), jnp.int32),
            pltpu.VMEM((1024, PAIRS), F32),
            pltpu.VMEM((1024, PAIRS), F32),
            pltpu.VMEM((6, 1024, WIDE), F32),
            pltpu.VMEM((2 * PAIRS, 1024), BF16),
            pltpu.VMEM((2 * PAIRS, 1024), BF16),
            pltpu.VMEM((2, HALF_BLOCKS, PAIRS, 128), F32),
            pltpu.VMEM((2, 3, PAIRS, WIDE), F32),
            pltpu.VMEM((2, 4, HALF_BLOCKS, 32, 128), F32),
            pltpu.VMEM((4, 4, 8, 128), jnp.int32),
            pltpu.VMEM((8, 8, 128), jnp.int32),
            pltpu.VMEM((2, 3, PAIRS, WIDE), F32),
            pltpu.VMEM((2, 3, PAIRS, WIDE), F32),
            dma((3,)), dma((6,)), dma((2, 3)), dma((2, 3)), dma((2, 3)), dma((2, 3)), dma((2,)),
            dma((3, 2, 3)), dma((3, 2, 3)),
            dma((2, 3)), dma((2, 3)), dma((7,)), dma((7,)),
        ],
        compiler_params=pltpu.CompilerParams(collective_id=0, has_side_effects=True, vmem_limit_bytes=62 << 20),
    )(tile_map, three_centre, occupied, virtual)


def join(cap, number, table, v2, op):
    any_space = pl.BlockSpec(memory_space=pl.ANY)
    dma = pltpu.SemaphoreType.DMA
    return pl.pallas_call(
        functools.partial(join_kernel, cap),
        name=f"join{cap}",
        out_shape=(
            jax.ShapeDtypeStruct((3 * WIDE, 6 * WIDE), F32),
            jax.ShapeDtypeStruct((2, 4, 3, WIDE, 128), BF16),
            jax.ShapeDtypeStruct((2, 4, 3, WIDE, 128), BF16),
            jax.ShapeDtypeStruct((2, 512, 3 * WIDE), BF16),
            jax.ShapeDtypeStruct((2, 512, 3 * WIDE), BF16),
        ),
        in_specs=[any_space] * 3,
        out_specs=(any_space,) * 5,
        scratch_shapes=[pltpu.SMEM((4, TILES), jnp.int32), pltpu.VMEM((2, TILES, 8, 128), F32)]
        + [pltpu.VMEM((cap + 1, 8, 128), F32)] * 32
        + [
            pltpu.VMEM((3, 2, 4, 2, PAIRS, WIDE), F32),
            pltpu.VMEM((3, 16, WIDE, 128), BF16),
            pltpu.VMEM((3, 16, WIDE, 128), BF16),
            pltpu.VMEM((2, 2, 512, 3 * WIDE), BF16),
            pltpu.VMEM((2, 2, 512, 3 * WIDE), BF16),
            pltpu.VMEM((3 * WIDE, 6 * WIDE), F32),
            dma((2, 6)), dma((2, 6)), dma((2, 4, 6)), dma((2, 4, 6)),
            dma((3, 4)), dma((3, 4)), dma((3, 4)), dma((3, 4)), dma((3,)), dma((5,)), dma((2, 2, 4)), dma((2,)),
        ],
        compiler_params=pltpu.CompilerParams(
            collective_id=number, has_side_effects=True, vmem_limit_bytes=62 << 20
        ),
    )(table, v2, op)


def finish(acc, lh, ll, rh, rl):
    tile = pl.BlockSpec((WIDE, 3 * WIDE), lambda h, i: (i, h))
    left = pl.BlockSpec((1, 4, 1, WIDE, 128), lambda h, i: (h, 0, i, 0, 0))
    right = pl.BlockSpec((1, 512, 3 * WIDE), lambda h, i: (h, 0, 0))
    return pl.pallas_call(
        finish_kernel,
        name="finish",
        grid=(2, 3),
        out_shape=jax.ShapeDtypeStruct((3 * WIDE, 6 * WIDE), F32),
        in_specs=[tile, left, left, right, right],
        out_specs=tile,
        compiler_params=pltpu.CompilerParams(vmem_limit_bytes=40 << 20),
    )(acc, lh, ll, rh, rl)


def tables(maps):
    kept = maps[:, 0, : 2 * HALF_BLOCKS].reshape(16, 2, HALF_BLOCKS).transpose(1, 0, 2).reshape(2, TILES)
    order = jnp.arange(TILES, dtype=jnp.int32)
    before = (order[None, :] < order[:, None]).astype(jnp.int32)
    pos = jnp.where(kept == 1, jnp.sum(kept[:, None, :] * before[None], axis=2), TILES)
    hit = pos[:, None, :] == order[None, :, None]
    idx = jnp.sum(jnp.where(hit, order[None, None, :], 0), axis=2)
    return jnp.concatenate([idx, pos], axis=0)


def body(three_centre, occupied, virtual, tile_map):
    v2, op, maps, chosen = spread(tile_map, three_centre[0], occupied[0], virtual[0])
    table = tables(maps)
    branches = [functools.partial(join, cap, i + 1) for i, cap in enumerate(CAPS)]
    return finish(*lax.switch(chosen[0], branches, table, v2.reshape(2, TILES, 8, 128), op))


def solution(mesh):
    return jax.shard_map(
        body,
        mesh=mesh,
        in_specs=(
            P("row", None, "col"),
            P("row", None, None),
            P("row", None, None),
            P("row", "col"),
        ),
        out_specs=P("row", "col"),
        check_vma=False,
    )
```
